512 devices in a mesh: pipe: 32 (over x, y), tensor: 16 (over z, core).
Axes of the slice: x: 4, y: 8, z: 8, core: 2. Of those that a mesh axis runs over, the one named last changes fastest.
Arguments:
- residual: bfloat16 [256, 8192], P(None, 'pipe'), may hold values from -22 to 22
- norm_gain: bfloat16 [8192], P('pipe'), may hold values from 0.099609375 to 1.8984375
- gate_codes: int32 [4096, 26624], P('pipe', 'tensor'), may hold values from 0 to 255
- gate_scales: bfloat16 [64, 26624], P('pipe', 'tensor'), may hold values from 0.0012130737 to 0.004852295
- up_codes: int32 [4096, 26624], P('pipe', 'tensor'), may hold values from 0 to 255
- up_scales: bfloat16 [64, 26624], P('pipe', 'tensor'), may hold values from 0.0012130737 to 0.004852295
- down_codes: int32 [13312, 8192], P('tensor', 'pipe'), may hold values from 0 to 255
- down_scales: bfloat16 [208, 8192], P('tensor', 'pipe'), may hold values from 0.0008544922 to 0.0034179688
- hidden_signs: int32 [26624], P('tensor'), may hold values from 0 to 1
Outputs:
- layer_out: bfloat16 [256, 8192], P(None, 'pipe')
The draws below stay inside these ranges and needn't reach their ends.
All inputs are finite; a program needn't handle non-finite values.
Results may differ from the reference program's by a relative error of at most 0.0075.
Values may be sent and summed in bfloat16 or wider, within the bound.
No kernel may reach another device: no remote copies, remote signals or barrier semaphores. Data moves between devices by JAX's collectives and lax.ppermute only.
A program may use at most 64 MiB of HBM per device.

```python
import math
import jax
import jax.numpy as jnp
from jax import lax

D = 8192
FF = 26624
GROUP = 128
FACTOR = 128
ROWS = 256
N_TENSOR = 16


def draw_residual(key, part):
    first, second = jax.random.split(key, 2)
    row_scale = jnp.exp(jax.random.uniform(second, (ROWS, 1), jnp.float32, math.log(0.3), math.log(3.0)))
    position = jnp.arange(D, dtype=jnp.float32) / D
    base = jnp.clip(jax.random.normal(first, (ROWS, D), jnp.float32), -4.0, 4.0)
    column_scale = 0.6 * jnp.exp(math.log(3.0) * position)
    return (base * row_scale * column_scale[None, :]).astype(jnp.bfloat16)


def with_ends(drawn, stream_key, least, top_value):
    shape = drawn.shape
    index_at = [jax.random.randint(jax.random.fold_in(stream_key, axis), (), 0, shape[axis]) for axis in range(len(shape))]
    drawn = drawn.at[tuple(index_at)].set(least)
    longest = shape.index(max(shape))
    index_at[longest] = (index_at[longest] + 1) % shape[longest]
    return drawn.at[tuple(index_at)].set(top_value)


def levels(own_key, dims, pieces, smallest, top_value):
    def one(dim, shards_of):
        steps = jax.random.uniform(jax.random.fold_in(jax.random.fold_in(own_key, 6), dim), (shards_of,), jnp.float32, smallest / len(pieces), top_value / len(pieces))
        return jnp.repeat(jnp.exp(steps), dims[dim] // shards_of).reshape((-1,) + (1,) * (len(dims) - dim - 1))

    factor_of = one(*pieces[0])
    for cut in pieces[1:]:
        factor_of = factor_of * one(*cut)
    return factor_of


def setup_inputs(seed: int = 0) -> dict:
    seeds = jax.random.split(jax.random.key(seed), 10)
    residual = draw_residual(jax.random.fold_in(seeds[9], 71), 0)
    norm_gain = jnp.clip(1.0 + 0.18 * jax.random.normal(seeds[1], (D,), jnp.float32), 0.099609375, 1.8984375).astype(jnp.bfloat16)
    gate_codes = with_ends(jax.random.randint(seeds[2], (D // 2, FF), 0, 256), jax.random.fold_in(seeds[2], 1), 0, 255).astype(jnp.int32)
    gate_scales = jnp.clip(jnp.exp(math.log(0.004852295) - 1.3862944 * jax.random.uniform(seeds[3], (D // GROUP, FF), jnp.float32) ** levels(seeds[3], (D // GROUP, FF), ((0, 32), (1, 16)), -0.2, 0.2)), 0.0012130737, 0.004852295).astype(jnp.bfloat16)
    up_codes = with_ends(jax.random.randint(seeds[4], (D // 2, FF), 0, 256), jax.random.fold_in(seeds[4], 1), 0, 255).astype(jnp.int32)
    up_scales = jnp.clip(jnp.exp(math.log(0.004852295) - 1.3862944 * jax.random.uniform(seeds[5], (D // GROUP, FF), jnp.float32) ** levels(seeds[5], (D // GROUP, FF), ((0, 32), (1, 16)), -0.2, 0.2)), 0.0012130737, 0.004852295).astype(jnp.bfloat16)
    down_codes = with_ends(jax.random.randint(seeds[6], (FF // 2, D), 0, 256), jax.random.fold_in(seeds[6], 1), 0, 255).astype(jnp.int32)
    down_scales = jnp.clip(jnp.exp(math.log(0.0034179688) - 1.3862944 * jax.random.uniform(seeds[7], (FF // GROUP, D), jnp.float32) ** levels(seeds[7], (FF // GROUP, D), ((0, 16), (1, 32)), -0.2, 0.2)), 0.0008544922, 0.0034179688).astype(jnp.bfloat16)
    hidden_signs = with_ends(jax.random.randint(seeds[8], (FF,), 0, 2), jax.random.fold_in(seeds[8], 1), 0, 1).astype(jnp.int32)
    return dict(residual=residual, norm_gain=norm_gain, gate_codes=gate_codes, gate_scales=gate_scales, up_codes=up_codes, up_scales=up_scales, down_codes=down_codes, down_scales=down_scales, hidden_signs=hidden_signs)


EPSILON = 1e-05

def walsh(dimension):
    indices = jnp.arange(dimension, dtype=jnp.int32)
    common_bits = jnp.bitwise_and(indices[:, None], indices[None, :])
    parity = jnp.zeros((dimension, dimension), jnp.int32)
    for shift_by in range(max(dimension.bit_length() - 1, 1)):
        parity = parity + jnp.bitwise_and(jnp.right_shift(common_bits, shift_by), 1)
    return (1 - 2 * jnp.bitwise_and(parity, 1)).astype(jnp.float32)

def dequantize(codes, scales):
    group_rows = 2 * codes.shape[0] // scales.shape[0]
    low_codes = jnp.bitwise_and(codes, 15)
    high_codes = jnp.right_shift(codes, 4)
    stacked = jnp.stack([low_codes, high_codes], axis=1).reshape(2 * codes.shape[0], codes.shape[1])
    spread_scales = jnp.repeat(scales.astype(jnp.float32), group_rows, axis=0)
    return ((stacked - 8).astype(jnp.float32) * spread_scales).astype(jnp.bfloat16)

def reference(residual, norm_gain, gate_codes, gate_scales, up_codes, up_scales, down_codes, down_scales, hidden_signs):
    residual_wide = residual.astype(jnp.float32)
    scaled_in = (residual_wide * norm_gain.astype(jnp.float32)[None, :]).astype(jnp.bfloat16)
    inverse = lax.rsqrt(lax.optimization_barrier(jnp.mean(residual_wide * residual_wide, axis=1)) + EPSILON)[:, None]
    gate = jnp.dot(scaled_in, dequantize(gate_codes, gate_scales), preferred_element_type=jnp.float32) * inverse
    up_value = jnp.dot(scaled_in, dequantize(up_codes, up_scales), preferred_element_type=jnp.float32) * inverse
    activated = (jax.nn.silu(gate) * up_value).astype(jnp.bfloat16)
    signed = activated.astype(jnp.float32) * (2 * hidden_signs - 1).astype(jnp.float32)[None, :]
    shaped = signed.reshape(ROWS, N_TENSOR, FF // N_TENSOR // FACTOR, FACTOR)
    rotated = jnp.einsum('st,rtbc,cd->rsbd', walsh(N_TENSOR), shaped, walsh(FACTOR), precision=lax.Precision.HIGHEST)
    rotated = (rotated.reshape(ROWS, FF) / math.sqrt(N_TENSOR * FACTOR)).astype(jnp.bfloat16)
    projected = jnp.dot(rotated, dequantize(down_codes, down_scales), preferred_element_type=jnp.float32)
    return (residual_wide + projected).astype(jnp.bfloat16)
```

```python
import jax
import jax.numpy as jnp
from jax import lax
from jax.experimental import pallas as pl
from jax.experimental.pallas import tpu as pltpu
from jax.sharding import Mesh
from jax.sharding import PartitionSpec as P

D = 8192
ROWS = 256
FACTOR = 128
EPSILON = 1e-05
NEAR = ("x", "yl")
FAR = ("yh", "t")
N_NEAR = 8
N_YH = 4
N_T = 16
LOCAL = 1664
SLICE = LOCAL // N_T
BLOCKS = LOCAL // FACTOR
WIDE = 2 * LOCAL + 128
F32 = jnp.float32
BF16 = jnp.bfloat16


def parity_sign(common):
    parity = common
    for shift in (4, 2, 1):
        parity = parity ^ (parity >> shift)
    return (1 - 2 * (parity & 1)).astype(F32)


def call(body, out_shape, scratch=()):
    return pl.pallas_call(
        body,
        out_shape=out_shape,
        scratch_shapes=scratch,
        compiler_params=pltpu.CompilerParams(vmem_limit_bytes=48 << 20),
    )


def project_in(x_ref, gain_ref, gate_codes, gate_scales, up_codes, up_scales, signs, out_ref):
    width = x_ref.shape[1]
    half = width // 2
    wide = x_ref[...].astype(F32)
    scaled = (wide * gain_ref[...].astype(F32)).astype(BF16)
    source = lax.broadcasted_iota(jnp.int32, (width, width), 0)
    target = lax.broadcasted_iota(jnp.int32, (width, width), 1)
    wanted = jnp.where(target < half, 2 * target, 2 * (target - half) + 1)
    order = (source == wanted).astype(F32).astype(BF16)
    ordered = jnp.dot(scaled, order, preferred_element_type=F32).astype(BF16)
    words = gate_codes.shape[0]
    top = lax.broadcasted_iota(jnp.int32, (words, FACTOR), 0) < words // 2

    for codes, scales, base in ((gate_codes, gate_scales, 0), (up_codes, up_scales, LOCAL)):
        for block in range(BLOCKS):
            lanes = pl.ds(block * FACTOR, FACTOR)
            word = codes[:, lanes]
            scale = scales[:, lanes].astype(F32)
            if base:
                scale = scale * (2 * signs[:, lanes] - 1).astype(F32)
            spread = jnp.where(top, scale[0:1, :], scale[1:2, :])
            low = (((word & 15) - 8).astype(F32) * spread).astype(BF16)
            high = (((word >> 4) - 8).astype(F32) * spread).astype(BF16)
            weight = jnp.concatenate([low, high], axis=0)
            part = jnp.dot(ordered, weight, preferred_element_type=F32)
            out_ref[:, pl.ds(base + block * FACTOR, FACTOR)] = part.astype(BF16)

    squares = jnp.sum(wide * wide, axis=1, keepdims=True)
    out_ref[:, pl.ds(2 * LOCAL, 128)] = two_parts(squares, ROWS)


def two_parts(value, rows):
    lane = lax.broadcasted_iota(jnp.int32, (rows, 128), 1)
    coarse = value.astype(BF16).astype(F32)
    fine = value - coarse
    return jnp.where(lane == 0, coarse, jnp.where(lane == 1, fine, 0.0)).astype(BF16)


def rotate_down(codes, scales, out_ref):
    row = lax.broadcasted_iota(jnp.int32, (FACTOR, FACTOR), 0)
    column = lax.broadcasted_iota(jnp.int32, (FACTOR, FACTOR), 1)
    half = FACTOR // 2
    column = jnp.where(column < half, 2 * column, 2 * (column - half) + 1)
    table = parity_sign(row & column).astype(BF16)
    norm = (N_T * FACTOR) ** -0.5
    for block in range(BLOCKS):
        word = codes[pl.ds(block * half, half), :]
        scale = scales[pl.ds(block, 1), :].astype(F32)
        low = (((word & 15) - 8).astype(F32) * scale).astype(BF16)
        high = (((word >> 4) - 8).astype(F32) * scale).astype(BF16)
        weight = jnp.concatenate([low, high], axis=0)
        mixed = jnp.dot(table, weight, preferred_element_type=F32) * norm
        out_ref[pl.ds(block * FACTOR, FACTOR), :] = mixed.astype(BF16)


def sum_near(parts, out_ref, total):
    rows = parts.shape[1]
    for block in range(WIDE // 128):
        lanes = pl.ds(block * 128, 128)
        value = parts[0, :, lanes].astype(F32)
        for source in range(1, N_NEAR):
            value = value + parts[source, :, lanes].astype(F32)
        total[:, lanes] = value
    squares = total[:, pl.ds(2 * LOCAL, 1)] + total[:, pl.ds(2 * LOCAL + 1, 1)]
    coarse = squares.astype(BF16).astype(F32)
    fine = squares - coarse
    lane = lax.broadcasted_iota(jnp.int32, (rows, 128), 1)
    for piece in range(N_T):
        gate = total[:, piece * SLICE : piece * SLICE + 128]
        gate = jnp.where(lane == SLICE, coarse, jnp.where(lane == SLICE + 1, fine, gate)).astype(BF16)
        up = total[:, LOCAL + piece * SLICE : LOCAL + piece * SLICE + 128].astype(BF16)
        for yh in range(N_YH):
            out_ref[yh * N_T + piece, :, 0:128] = gate[8 * yh : 8 * yh + 8, :]
            out_ref[yh * N_T + piece, :, 128:256] = up[8 * yh : 8 * yh + 8, :]


def activate(parts, out_ref):
    def summed(t):
        value = parts[t].astype(F32)
        for yh in range(1, N_YH):
            value = value + parts[yh * N_T + t].astype(F32)
        return value

    first = summed(0)
    squares = first[:, SLICE : SLICE + 1] + first[:, SLICE + 1 : SLICE + 2]
    inverse = lax.rsqrt(squares / D + EPSILON)
    values = []
    for t in range(N_T):
        both = first if t == 0 else summed(t)
        gate = both[:, 0:128] * inverse
        up = both[:, 128:256] * inverse
        act = gate / (1.0 + jnp.exp(-gate)) * up
        values.append(act.astype(BF16).astype(F32))
    step = 1
    while step < N_T:
        values = [
            values[i] + values[i + step] if not i & step else values[i - step] - values[i]
            for i in range(N_T)
        ]
        step *= 2
    for t in range(N_T):
        mixed = values[t].astype(BF16)
        for yh in range(N_YH):
            out_ref[yh * N_T + t] = mixed


def spread_near(parts, out_ref, joined):
    for piece in range(N_T):
        for yh in range(N_YH):
            joined[8 * yh : 8 * yh + 8, piece * SLICE : piece * SLICE + 128] = parts[yh * N_T + piece].astype(F32)
    for block in range(BLOCKS):
        lanes = pl.ds(block * 128, 128)
        value = joined[:, lanes].astype(BF16)
        for target in range(N_NEAR):
            out_ref[target, :, lanes] = value


def project_out(act, weight, out_ref):
    out_ref[...] = jnp.dot(act[...], weight[...], preferred_element_type=F32).astype(BF16)


def finish(here, parts, residual, out_ref):
    rows = ROWS // N_T
    value = parts[0].astype(F32)
    for t in range(1, N_T):
        value = value + parts[t].astype(F32)
    start = pl.multiple_of(here[0] * rows, rows)
    value = (value + residual[pl.ds(start, rows), :].astype(F32)).astype(BF16)
    for t in range(N_T):
        out_ref[t] = value


def exchange(blocks, axes):
    return lax.all_to_all(blocks, axes, split_axis=0, concat_axis=0, tiled=True)


def shards(residual, norm_gain, gate_codes, gate_scales, up_codes, up_scales, down_codes, down_scales, hidden_signs):
    shape = jax.ShapeDtypeStruct
    columns = residual.shape[1]
    part = call(project_in, shape((ROWS, WIDE), BF16))(
        residual, norm_gain[None, :], gate_codes, gate_scales, up_codes, up_scales, hidden_signs[None, :]
    )
    near_rows = ROWS // N_NEAR
    near = exchange(part.reshape(N_NEAR, near_rows, WIDE), NEAR)
    down_weight = call(rotate_down, shape((LOCAL, columns), BF16))(down_codes, down_scales)
    pieces = call(sum_near, shape((N_YH * N_T, 8, 256), BF16), [pltpu.VMEM((near_rows, WIDE), F32)])(near)
    far = exchange(pieces, FAR)
    mixed = call(activate, shape((N_YH * N_T, 8, 128), BF16))(far)
    back = exchange(mixed, FAR)
    copies = call(spread_near, shape((N_NEAR, near_rows, LOCAL), BF16), [pltpu.VMEM((near_rows, LOCAL + 128), F32)])(back)
    rotated = exchange(copies, NEAR).reshape(ROWS, LOCAL)
    partial = call(project_out, shape((ROWS, columns), BF16))(rotated, down_weight)
    sums = exchange(partial.reshape(N_T, ROWS // N_T, columns), "t")
    here = lax.axis_index("t").astype(jnp.int32).reshape(1)
    out = pl.pallas_call(
        finish,
        out_shape=shape((N_T, ROWS // N_T, columns), BF16),
        in_specs=[
            pl.BlockSpec(memory_space=pltpu.SMEM),
            pl.BlockSpec(memory_space=pltpu.VMEM),
            pl.BlockSpec(memory_space=pltpu.VMEM),
        ],
    )(here, sums, residual)
    return exchange(out, "t").reshape(ROWS, columns)


def solution(mesh):
    torus = Mesh(mesh.devices.reshape(4, N_YH, 2, N_T), ("x", "yh", "yl", "t"))
    pipe = ("x", "yh", "yl")
    placed = (
        P(None, pipe),
        P(pipe),
        P(pipe, "t"),
        P(pipe, "t"),
        P(pipe, "t"),
        P(pipe, "t"),
        P("t", pipe),
        P("t", pipe),
        P("t"),
    )
    return jax.shard_map(shards, mesh=torus, in_specs=placed, out_specs=P(None, pipe), check_vma=False)
```

```python
import jax
import jax.numpy as jnp
from jax import lax
from jax.experimental import pallas as pl
from jax.experimental.pallas import tpu as pltpu
from jax.sharding import Mesh
from jax.sharding import PartitionSpec as P

D = 8192
ROWS = 256
FACTOR = 128
EPSILON = 1e-05
NEAR = ("x", "yl")
FAR = ("yh", "zh")
TENSOR = ("zh", "zl", "c")
N_NEAR = 8
N_YH = 4
N_ZH = 4
N_T = 16
LOCAL = 1664
SLICE = LOCAL // N_ZH
BLOCKS = LOCAL // FACTOR
WIDE = 2 * LOCAL + 128
PIECE = 2 * SLICE + 64
NEAR_ROWS = ROWS // N_NEAR
OWN_ROWS = ROWS // N_T
F32 = jnp.float32
BF16 = jnp.bfloat16


def parity_sign(common):
    parity = common
    for shift in (4, 2, 1):
        parity = parity ^ (parity >> shift)
    return (1 - 2 * (parity & 1)).astype(F32)


def call(body, out_shape, scratch=()):
    return pl.pallas_call(
        body,
        out_shape=out_shape,
        scratch_shapes=scratch,
        compiler_params=pltpu.CompilerParams(vmem_limit_bytes=48 << 20),
    )


def two_parts(value, lanes):
    lane = lax.broadcasted_iota(jnp.int32, (value.shape[0], lanes), 1)
    coarse = value.astype(BF16).astype(F32)
    return jnp.where(lane == 0, coarse, jnp.where(lane == 1, value - coarse, 0.0))


def project_in(x_hbm, gain_hbm, gate_hbm, gate_scales_hbm, up_hbm, up_scales_hbm, signs_hbm, out_ref, own_ref, *scratch):
    x_ref, gain_ref, gate_codes, gate_scales, up_codes, up_scales, signs, sems = scratch
    small = [
        pltpu.make_async_copy(source, target, sems.at[i])
        for i, (source, target) in enumerate(
            [(x_hbm, x_ref), (gain_hbm, gain_ref), (gate_scales_hbm, gate_scales), (up_scales_hbm, up_scales), (signs_hbm, signs)]
        )
    ]
    for copy in small:
        copy.start()
    copies = {}
    starts = (0, 4, 7, 10, BLOCKS)
    slot = len(small)
    for which, (source, target) in enumerate(((gate_hbm, gate_codes), (up_hbm, up_codes))):
        for first, last in zip(starts[:-1], starts[1:]):
            lanes = pl.ds(first * FACTOR, (last - first) * FACTOR)
            copies[which, first] = pltpu.make_async_copy(source.at[:, lanes], target.at[:, lanes], sems.at[slot])
            copies[which, first].start()
            slot += 1

    width = x_ref.shape[1]
    half = width // 2
    source = lax.broadcasted_iota(jnp.int32, (width, width), 0)
    target = lax.broadcasted_iota(jnp.int32, (width, width), 1)
    wanted = jnp.where(target < half, 2 * target, 2 * (target - half) + 1)
    order = (source == wanted).astype(F32).astype(BF16)
    words = gate_codes.shape[0]
    top = lax.broadcasted_iota(jnp.int32, (words, FACTOR), 0) < words // 2
    my_t = (lax.axis_index("zh") * 2 + lax.axis_index("zl")) * 2 + lax.axis_index("c")
    for copy in small:
        copy.wait()
    wide = x_ref[...].astype(F32)
    scaled = (wide * gain_ref[...].reshape(1, width).astype(F32)).astype(BF16)
    ordered = jnp.dot(scaled, order, preferred_element_type=F32).astype(BF16)
    squares = jnp.sum(wide * wide, axis=1, keepdims=True)
    out_ref[:, pl.ds(2 * LOCAL, 128)] = two_parts(squares, 128).astype(BF16)
    own_ref[...] = x_ref[pl.ds(pl.multiple_of(my_t * OWN_ROWS, OWN_ROWS), OWN_ROWS), :]

    for which, (codes, scales, base) in enumerate(((gate_codes, gate_scales, 0), (up_codes, up_scales, LOCAL))):
        for block in range(BLOCKS):
            if (which, block) in copies:
                copies[which, block].wait()
            lanes = pl.ds(block * FACTOR, FACTOR)
            word = codes[:, lanes]
            scale = scales[:, lanes].astype(F32)
            if base:
                scale = scale * (2 * signs[lanes].reshape(1, FACTOR) - 1).astype(F32)
            spread = jnp.where(top, scale[0:1, :], scale[1:2, :])
            low = (((word & 15) - 8).astype(F32) * spread).astype(BF16)
            high = (((word >> 4) - 8).astype(F32) * spread).astype(BF16)
            weight = jnp.concatenate([low, high], axis=0)
            part = jnp.dot(ordered, weight, preferred_element_type=F32)
            out_ref[:, pl.ds(base + block * FACTOR, FACTOR)] = part.astype(BF16)


def rotate_down(codes, scales, out_ref):
    row = lax.broadcasted_iota(jnp.int32, (FACTOR, FACTOR), 0)
    column = lax.broadcasted_iota(jnp.int32, (FACTOR, FACTOR), 1)
    half = FACTOR // 2
    column = jnp.where(column < half, 2 * column, 2 * (column - half) + 1)
    table = parity_sign(row & column).astype(BF16)
    norm = (N_T * FACTOR) ** -0.5
    for block in range(BLOCKS):
        word = codes[pl.ds(block * half, half), :]
        scale = scales[pl.ds(block, 1), :].astype(F32)
        low = (((word & 15) - 8).astype(F32) * scale).astype(BF16)
        high = (((word >> 4) - 8).astype(F32) * scale).astype(BF16)
        weight = jnp.concatenate([low, high], axis=0)
        mixed = jnp.dot(table, weight, preferred_element_type=F32) * norm
        out_ref[pl.ds(block * FACTOR, FACTOR), :] = mixed.astype(BF16)


def sum_near(parts, out_ref, total, joined):
    for block in range(WIDE // 128):
        lanes = pl.ds(block * 128, 128)
        value = parts[0, :, lanes].astype(F32)
        for source in range(1, N_NEAR):
            value = value + parts[source, :, lanes].astype(F32)
        total[:, lanes] = value
    squares = total[:, pl.ds(2 * LOCAL, 1)] + total[:, pl.ds(2 * LOCAL + 1, 1)]
    tail = two_parts(squares, 64)
    for piece in range(N_ZH):
        joined[:, 0:SLICE] = total[:, piece * SLICE : (piece + 1) * SLICE]
        joined[:, SLICE : 2 * SLICE] = total[:, LOCAL + piece * SLICE : LOCAL + (piece + 1) * SLICE]
        joined[:, 2 * SLICE : PIECE] = tail
        value = joined[...].astype(BF16)
        for yh in range(N_YH):
            out_ref[yh * N_ZH + piece] = value[8 * yh : 8 * yh + 8, :]


def activate(parts, out_ref, joined):
    values = []
    inverse = None
    for z in range(N_ZH):
        value = parts[z].astype(F32)
        for yh in range(1, N_YH):
            value = value + parts[yh * N_ZH + z].astype(F32)
        joined[...] = value
        if z == 0:
            squares = joined[:, 2 * SLICE : 2 * SLICE + 1] + joined[:, 2 * SLICE + 1 : 2 * SLICE + 2]
            inverse = lax.rsqrt(squares / D + EPSILON)
        gate = joined[:, 0:SLICE] * inverse
        up = joined[:, SLICE : 2 * SLICE] * inverse
        act = gate / (1.0 + jnp.exp(-gate)) * up
        values.append(act.astype(BF16).astype(F32))
    step = 1
    while step < N_ZH:
        values = [
            values[i] + values[i + step] if not i & step else values[i - step] - values[i]
            for i in range(N_ZH)
        ]
        step *= 2
    for z in range(N_ZH):
        mixed = values[z].astype(BF16)
        for yh in range(N_YH):
            out_ref[yh * N_ZH + z] = mixed


def spread_near(parts, out_ref, joined):
    for piece in range(N_ZH):
        for yh in range(N_YH):
            joined[8 * yh : 8 * yh + 8, piece * SLICE : (piece + 1) * SLICE] = parts[yh * N_ZH + piece].astype(F32)
    for block in range(BLOCKS):
        lanes = pl.ds(block * 128, 128)
        value = joined[:, lanes].astype(BF16)
        for target in range(N_NEAR):
            out_ref[target, :, lanes] = value


def project_out(act, weight, out_ref):
    out_ref[...] = jnp.dot(act[...], weight[...], preferred_element_type=F32).astype(BF16)


def finish(parts, residual, out_ref):
    value = residual[...].astype(F32)
    for t in range(N_T):
        value = value + parts[t].astype(F32)
    value = value.astype(BF16)
    for t in range(N_T):
        out_ref[t] = value


def exchange(blocks, axes):
    return lax.all_to_all(blocks, axes, split_axis=0, concat_axis=0, tiled=True)


def blend(axis, own_ref, other_ref, out_ref):
    sign = (1 - 2 * lax.axis_index(axis)).astype(F32)
    out_ref[...] = (own_ref[...].astype(F32) * sign + other_ref[...].astype(F32)).astype(BF16)


def pair_mixed(weight, axis):
    other = lax.ppermute(weight, axis, [(0, 1), (1, 0)])
    return call(lambda *refs: blend(axis, *refs), jax.ShapeDtypeStruct(weight.shape, BF16))(weight, other)


def shards(residual, norm_gain, gate_codes, gate_scales, up_codes, up_scales, down_codes, down_scales, hidden_signs):
    shape = jax.ShapeDtypeStruct
    columns = residual.shape[1]
    inputs = (residual, norm_gain, gate_codes, gate_scales, up_codes, up_scales, hidden_signs)
    part, own_rows = pl.pallas_call(
        project_in,
        out_shape=[shape((ROWS, WIDE), BF16), shape((OWN_ROWS, columns), BF16)],
        in_specs=[pl.BlockSpec(memory_space=pltpu.HBM)] * len(inputs),
        scratch_shapes=[pltpu.VMEM(a.shape, a.dtype) for a in inputs] + [pltpu.SemaphoreType.DMA((13,))],
        compiler_params=pltpu.CompilerParams(vmem_limit_bytes=48 << 20),
    )(*(pltpu.with_memory_space_constraint(a, pltpu.HBM) for a in inputs))
    near = exchange(part.reshape(N_NEAR, NEAR_ROWS, WIDE), NEAR)
    weight = call(rotate_down, shape((LOCAL, columns), BF16))(down_codes, down_scales)
    weight = pair_mixed(pair_mixed(weight, "c"), "zl")
    scratch = [pltpu.VMEM((NEAR_ROWS, WIDE), F32), pltpu.VMEM((NEAR_ROWS, PIECE), F32)]
    pieces = call(sum_near, shape((N_YH * N_ZH, 8, PIECE), BF16), scratch)(near)
    far = exchange(pieces, FAR)
    mixed = call(activate, shape((N_YH * N_ZH, 8, SLICE), BF16), [pltpu.VMEM((8, PIECE), F32)])(far)
    back = exchange(mixed, FAR)
    copies = call(spread_near, shape((N_NEAR, NEAR_ROWS, LOCAL), BF16), [pltpu.VMEM((NEAR_ROWS, LOCAL), F32)])(back)
    rotated = exchange(copies, NEAR).reshape(ROWS, LOCAL)
    partial = call(project_out, shape((ROWS, columns), BF16))(rotated, weight)
    sums = exchange(partial.reshape(N_T, OWN_ROWS, columns), TENSOR)
    out = call(finish, shape((N_T, OWN_ROWS, columns), BF16))(sums, own_rows)
    return exchange(out, TENSOR).reshape(ROWS, columns)


def solution(mesh):
    torus = Mesh(mesh.devices.reshape(4, N_YH, 2, N_ZH, 2, 2), ("x", "yh", "yl", "zh", "zl", "c"))
    pipe = ("x", "yh", "yl")
    placed = (
        P(None, pipe),
        P(pipe),
        P(pipe, TENSOR),
        P(pipe, TENSOR),
        P(pipe, TENSOR),
        P(pipe, TENSOR),
        P(TENSOR, pipe),
        P(TENSOR, pipe),
        P(TENSOR),
    )
    return jax.shard_map(shards, mesh=torus, in_specs=placed, out_specs=P(None, pipe), check_vma=False)
```

```python
import jax
import jax.numpy as jnp
from jax import lax
from jax.experimental import pallas as pl
from jax.experimental.pallas import tpu as pltpu
from jax.sharding import Mesh
from jax.sharding import PartitionSpec as P

D = 8192
ROWS = 256
FACTOR = 128
EPSILON = 1e-05
NEAR = ("x", "yl")
FAR = ("yh", "zh")
TENSOR = ("zh", "zl", "c")
N_NEAR = 8
N_YH = 4
N_ZH = 4
N_T = 16
LOCAL = 1664
SLICE = LOCAL // N_ZH
BLOCKS = LOCAL // FACTOR
WIDE = 2 * LOCAL + 128
PIECE = 2 * SLICE + 64
NEAR_ROWS = ROWS // N_NEAR
OWN_ROWS = ROWS // N_T
F32 = jnp.float32
BF16 = jnp.bfloat16


def parity_sign(common):
    parity = common
    for shift in (4, 2, 1):
        parity = parity ^ (parity >> shift)
    return (1 - 2 * (parity & 1)).astype(F32)


def call(body, out_shape, scratch=()):
    return pl.pallas_call(
        body,
        out_shape=out_shape,
        scratch_shapes=scratch,
        compiler_params=pltpu.CompilerParams(vmem_limit_bytes=48 << 20),
    )


def two_parts(value, lanes):
    lane = lax.broadcasted_iota(jnp.int32, (value.shape[0], lanes), 1)
    coarse = value.astype(BF16).astype(F32)
    return jnp.where(lane == 0, coarse, jnp.where(lane == 1, value - coarse, 0.0))


def project_in(x_hbm, gain_hbm, gate_hbm, gate_scales_hbm, up_hbm, up_scales_hbm, signs_hbm, out_hbm, own_ref, *scratch):
    out_ref, out_sems, x_ref, gain_ref, gate_codes, gate_scales, up_codes, up_scales, signs, sems = scratch
    small = [
        pltpu.make_async_copy(source, target, sems.at[i])
        for i, (source, target) in enumerate(
            [(x_hbm, x_ref), (gain_hbm, gain_ref), (gate_scales_hbm, gate_scales), (up_scales_hbm, up_scales), (signs_hbm, signs)]
        )
    ]
    for copy in small:
        copy.start()
    copies = {}
    starts = (0, 4, 7, 10, BLOCKS)
    slot = len(small)
    for which, (source, target) in enumerate(((gate_hbm, gate_codes), (up_hbm, up_codes))):
        for first, last in zip(starts[:-1], starts[1:]):
            lanes = pl.ds(first * FACTOR, (last - first) * FACTOR)
            copies[which, first] = pltpu.make_async_copy(source.at[:, lanes], target.at[:, lanes], sems.at[slot])
            copies[which, first].start()
            slot += 1

    width = x_ref.shape[1]
    half = width // 2
    source = lax.broadcasted_iota(jnp.int32, (width, width), 0)
    target = lax.broadcasted_iota(jnp.int32, (width, width), 1)
    wanted = jnp.where(target < half, 2 * target, 2 * (target - half) + 1)
    order = (source == wanted).astype(F32).astype(BF16)
    words = gate_codes.shape[0]
    top = lax.broadcasted_iota(jnp.int32, (words, FACTOR), 0) < words // 2
    my_t = (lax.axis_index("zh") * 2 + lax.axis_index("zl")) * 2 + lax.axis_index("c")
    for copy in small:
        copy.wait()
    wide = x_ref[...].astype(F32)
    scaled = (wide * gain_ref[...].reshape(1, width).astype(F32)).astype(BF16)
    ordered = jnp.dot(scaled, order, preferred_element_type=F32).astype(BF16)
    squares = jnp.sum(wide * wide, axis=1, keepdims=True)
    out_ref[:, pl.ds(2 * LOCAL, 128)] = two_parts(squares, 128).astype(BF16)
    leaving = []

    def leave(first, width):
        lanes = pl.ds(first, width)
        leaving.append(pltpu.make_async_copy(out_ref.at[:, lanes], out_hbm.at[:, lanes], out_sems.at[len(leaving)]))
        leaving[-1].start()

    leave(2 * LOCAL, 128)
    own_ref[...] = x_ref[pl.ds(pl.multiple_of(my_t * OWN_ROWS, OWN_ROWS), OWN_ROWS), :]

    for which, (codes, scales, base) in enumerate(((gate_codes, gate_scales, 0), (up_codes, up_scales, LOCAL))):
        for block in range(BLOCKS):
            if (which, block) in copies:
                copies[which, block].wait()
            lanes = pl.ds(block * FACTOR, FACTOR)
            word = codes[:, lanes]
            scale = scales[:, lanes].astype(F32)
            if base:
                scale = scale * (2 * signs[lanes].reshape(1, FACTOR) - 1).astype(F32)
            spread = jnp.where(top, scale[0:1, :], scale[1:2, :])
            low = (((word & 15) - 8).astype(F32) * spread).astype(BF16)
            high = (((word >> 4) - 8).astype(F32) * spread).astype(BF16)
            weight = jnp.concatenate([low, high], axis=0)
            part = jnp.dot(ordered, weight, preferred_element_type=F32)
            out_ref[:, pl.ds(base + block * FACTOR, FACTOR)] = part.astype(BF16)
            if block + 1 in starts:
                first = starts[starts.index(block + 1) - 1]
                leave(base + first * FACTOR, (block + 1 - first) * FACTOR)
    for copy in leaving:
        copy.wait()


def rotate_down(codes, scales, out_ref):
    row = lax.broadcasted_iota(jnp.int32, (FACTOR, FACTOR), 0)
    column = lax.broadcasted_iota(jnp.int32, (FACTOR, FACTOR), 1)
    half = FACTOR // 2
    column = jnp.where(column < half, 2 * column, 2 * (column - half) + 1)
    table = parity_sign(row & column).astype(BF16)
    norm = (N_T * FACTOR) ** -0.5
    for block in range(BLOCKS):
        word = codes[pl.ds(block * half, half), :]
        scale = scales[pl.ds(block, 1), :].astype(F32)
        low = (((word & 15) - 8).astype(F32) * scale).astype(BF16)
        high = (((word >> 4) - 8).astype(F32) * scale).astype(BF16)
        weight = jnp.concatenate([low, high], axis=0)
        mixed = jnp.dot(table, weight, preferred_element_type=F32) * norm
        out_ref[pl.ds(block * FACTOR, FACTOR), :] = mixed.astype(BF16)


def sum_near(parts, out_ref, total, joined):
    for block in range(WIDE // 128):
        lanes = pl.ds(block * 128, 128)
        value = parts[0, :, lanes].astype(F32)
        for source in range(1, N_NEAR):
            value = value + parts[source, :, lanes].astype(F32)
        total[:, lanes] = value
    squares = total[:, pl.ds(2 * LOCAL, 1)] + total[:, pl.ds(2 * LOCAL + 1, 1)]
    tail = two_parts(squares, 64)
    for piece in range(N_ZH):
        joined[:, 0:SLICE] = total[:, piece * SLICE : (piece + 1) * SLICE]
        joined[:, SLICE : 2 * SLICE] = total[:, LOCAL + piece * SLICE : LOCAL + (piece + 1) * SLICE]
        joined[:, 2 * SLICE : PIECE] = tail
        value = joined[...].astype(BF16)
        for yh in range(N_YH):
            out_ref[yh * N_ZH + piece] = value[8 * yh : 8 * yh + 8, :]


def source_of(shift):
    return lax.rem(lax.axis_index("zh") + N_ZH - shift, N_ZH)


def activate(parts, out_ref, joined, mixed, ordered):
    values = []
    inverse = None
    for z in range(N_ZH):
        value = parts[z].astype(F32)
        for yh in range(1, N_YH):
            value = value + parts[yh * N_ZH + z].astype(F32)
        joined[...] = value
        if z == 0:
            squares = joined[:, 2 * SLICE : 2 * SLICE + 1] + joined[:, 2 * SLICE + 1 : 2 * SLICE + 2]
            inverse = lax.rsqrt(squares / D + EPSILON)
        gate = joined[:, 0:SLICE] * inverse
        up = joined[:, SLICE : 2 * SLICE] * inverse
        act = gate / (1.0 + jnp.exp(-gate)) * up
        values.append(act.astype(BF16).astype(F32))
    step = 1
    while step < N_ZH:
        values = [
            values[i] + values[i + step] if not i & step else values[i - step] - values[i]
            for i in range(N_ZH)
        ]
        step *= 2
    for z in range(N_ZH):
        mixed[z] = values[z]
    for j in range(N_ZH):
        ordered[:, j * SLICE : (j + 1) * SLICE] = mixed[source_of(j)]
    for block in range(BLOCKS):
        lanes = pl.ds(block * 128, 128)
        value = ordered[:, lanes].astype(BF16)
        for target in range(out_ref.shape[0]):
            out_ref[target, :, lanes] = value


def spread_near(parts, out_ref):
    for yh in range(N_YH):
        value = parts[yh]
        for target in range(N_NEAR):
            out_ref[target, 8 * yh : 8 * yh + 8, :] = value


def project_out(act, *refs):
    weights, (out_ref, joined) = refs[:N_ZH], refs[N_ZH:]
    for j in range(N_ZH):
        joined[pl.ds(j * SLICE, SLICE), :] = weights[j][...]
    out_ref[...] = jnp.dot(act[...], joined[...], preferred_element_type=F32).astype(BF16)


def finish(parts, residual, out_ref):
    value = residual[...].astype(F32)
    for t in range(N_T):
        value = value + parts[t].astype(F32)
    value = value.astype(BF16)
    for t in range(N_T):
        out_ref[t] = value


def exchange(blocks, axes):
    return lax.all_to_all(blocks, axes, split_axis=0, concat_axis=0, tiled=True)


def blended(axis, own, other):
    sign = (1 - 2 * lax.axis_index(axis)).astype(F32)
    return (own.astype(F32) * sign + other.astype(F32)).astype(BF16)


def swapped(weight, axis):
    return lax.ppermute(weight, axis, [(0, 1), (1, 0)])


def blend_core(own_ref, other_ref, out_ref):
    out_ref[...] = blended("c", own_ref[...], other_ref[...])


def blend_chip(own_ref, other_ref, *out_refs):
    for j in range(N_ZH):
        group = lax.rem(lax.axis_index("zh") + j, N_ZH)
        rows = pl.ds(pl.multiple_of(group * SLICE, SLICE), SLICE)
        out_refs[j][...] = blended("zl", own_ref[rows, :], other_ref[rows, :])


def shards(residual, norm_gain, gate_codes, gate_scales, up_codes, up_scales, down_codes, down_scales, hidden_signs):
    shape = jax.ShapeDtypeStruct
    columns = residual.shape[1]
    inputs = (residual, norm_gain, gate_codes, gate_scales, up_codes, up_scales, hidden_signs)
    part, own_rows = pl.pallas_call(
        project_in,
        out_shape=[shape((ROWS, WIDE), BF16), shape((OWN_ROWS, columns), BF16)],
        in_specs=[pl.BlockSpec(memory_space=pltpu.HBM)] * len(inputs),
        out_specs=[pl.BlockSpec(memory_space=pltpu.HBM), pl.BlockSpec(memory_space=pltpu.VMEM)],
        scratch_shapes=[pltpu.VMEM((ROWS, WIDE), BF16), pltpu.SemaphoreType.DMA((9,))]
        + [pltpu.VMEM(a.shape, a.dtype) for a in inputs] + [pltpu.SemaphoreType.DMA((13,))],
        compiler_params=pltpu.CompilerParams(vmem_limit_bytes=48 << 20),
    )(*(pltpu.with_memory_space_constraint(a, pltpu.HBM) for a in inputs))
    near = exchange(part.reshape(N_NEAR, NEAR_ROWS, WIDE), NEAR)
    weight = call(rotate_down, shape((LOCAL, columns), BF16))(down_codes, down_scales)
    other = swapped(weight, "c")
    weight = call(blend_core, shape(weight.shape, BF16))(weight, other)
    other = swapped(weight, "zl")
    groups = call(blend_chip, [shape((SLICE, columns), BF16)] * N_ZH)(weight, other)
    weights = [groups[0]]
    for j in range(1, N_ZH):
        weights.append(lax.ppermute(groups[j], "zh", [(i, (i + j) % N_ZH) for i in range(N_ZH)]))
    scratch = [pltpu.VMEM((NEAR_ROWS, WIDE), F32), pltpu.VMEM((NEAR_ROWS, PIECE), F32)]
    pieces = call(sum_near, shape((N_YH * N_ZH, 8, PIECE), BF16), scratch)(near)
    far = exchange(pieces, FAR)
    scratch = [pltpu.VMEM((8, PIECE), F32), pltpu.VMEM((N_ZH, 8, SLICE), F32), pltpu.VMEM((8, LOCAL), F32)]
    mixed = call(activate, shape((N_YH, 8, LOCAL), BF16), scratch)(far)
    back = exchange(mixed, "yh")
    copies = call(spread_near, shape((N_NEAR, NEAR_ROWS, LOCAL), BF16))(back)
    rotated = exchange(copies, NEAR).reshape(ROWS, LOCAL)
    partial = call(project_out, shape((ROWS, columns), BF16), [pltpu.VMEM((LOCAL, columns), BF16)])(rotated, *weights)
    sums = exchange(partial.reshape(N_T, OWN_ROWS, columns), TENSOR)
    out = call(finish, shape((N_T, OWN_ROWS, columns), BF16))(sums, own_rows)
    return exchange(out, TENSOR).reshape(ROWS, columns)


def solution(mesh):
    torus = Mesh(mesh.devices.reshape(4, N_YH, 2, N_ZH, 2, 2), ("x", "yh", "yl", "zh", "zl", "c"))
    pipe = ("x", "yh", "yl")
    placed = (
        P(None, pipe),
        P(pipe),
        P(pipe, TENSOR),
        P(pipe, TENSOR),
        P(pipe, TENSOR),
        P(pipe, TENSOR),
        P(TENSOR, pipe),
        P(TENSOR, pipe),
        P(TENSOR),
    )
    return jax.shard_map(shards, mesh=torus, in_specs=placed, out_specs=P(None, pipe), check_vma=False)
```

```python
import jax
import jax.numpy as jnp
from jax import lax
from jax.experimental import pallas as pl
from jax.experimental.pallas import tpu as pltpu
from jax.sharding import Mesh
from jax.sharding import PartitionSpec as P

D = 8192
ROWS = 256
FACTOR = 128
EPSILON = 1e-05
NEAR = ("x", "yl")
FAR = ("yh", "zh")
TENSOR = ("zh", "zl", "c")
N_NEAR = 8
N_YH = 4
N_ZH = 4
N_T = 16
LOCAL = 1664
SLICE = LOCAL // N_ZH
BLOCKS = LOCAL // FACTOR
WIDE = 2 * LOCAL + 128
PIECE = 2 * SLICE + 64
NEAR_ROWS = ROWS // N_NEAR
OWN_ROWS = ROWS // N_T
F32 = jnp.float32
BF16 = jnp.bfloat16


def parity_sign(common):
    parity = common
    for shift in (4, 2, 1):
        parity = parity ^ (parity >> shift)
    return (1 - 2 * (parity & 1)).astype(F32)


def call(body, out_shape, scratch=()):
    return pl.pallas_call(
        body,
        out_shape=out_shape,
        scratch_shapes=scratch,
        compiler_params=pltpu.CompilerParams(vmem_limit_bytes=48 << 20),
    )


def two_parts(value, lanes):
    lane = lax.broadcasted_iota(jnp.int32, (value.shape[0], lanes), 1)
    coarse = value.astype(BF16).astype(F32)
    return jnp.where(lane == 0, coarse, jnp.where(lane == 1, value - coarse, 0.0))


def project_in(x_hbm, gain_hbm, gate_hbm, gate_scales_hbm, up_hbm, up_scales_hbm, signs_hbm, out_hbm, own_ref, *scratch):
    out_ref, out_sems, x_ref, gain_ref, gate_codes, gate_scales, up_codes, up_scales, signs, sems = scratch
    small = [
        pltpu.make_async_copy(source, target, sems.at[i])
        for i, (source, target) in enumerate(
            [(x_hbm, x_ref), (gain_hbm, gain_ref), (gate_scales_hbm, gate_scales), (up_scales_hbm, up_scales), (signs_hbm, signs)]
        )
    ]
    for copy in small:
        copy.start()
    copies = {}
    starts = (0, BLOCKS)
    ends = (0, 7, BLOCKS)
    slot = len(small)
    for which, (source, target) in enumerate(((gate_hbm, gate_codes), (up_hbm, up_codes))):
        for first, last in zip(starts[:-1], starts[1:]):
            lanes = pl.ds(first * FACTOR, (last - first) * FACTOR)
            copies[which, first] = pltpu.make_async_copy(source.at[:, lanes], target.at[:, lanes], sems.at[slot])
            copies[which, first].start()
            slot += 1

    width = x_ref.shape[1]
    half = width // 2
    source = lax.broadcasted_iota(jnp.int32, (width, width), 0)
    target = lax.broadcasted_iota(jnp.int32, (width, width), 1)
    wanted = jnp.where(target < half, 2 * target, 2 * (target - half) + 1)
    order = (source == wanted).astype(F32).astype(BF16)
    words = gate_codes.shape[0]
    top = lax.broadcasted_iota(jnp.int32, (words, FACTOR), 0) < words // 2
    my_t = (lax.axis_index("zh") * 2 + lax.axis_index("zl")) * 2 + lax.axis_index("c")
    for copy in small:
        copy.wait()
    wide = x_ref[...].astype(F32)
    scaled = (wide * gain_ref[...].reshape(1, width).astype(F32)).astype(BF16)
    ordered = jnp.dot(scaled, order, preferred_element_type=F32).astype(BF16)
    squares = jnp.sum(wide * wide, axis=1, keepdims=True)
    out_ref[:, pl.ds(2 * LOCAL, 128)] = two_parts(squares, 128).astype(BF16)
    leaving = []

    def leave(first, width):
        lanes = pl.ds(first, width)
        leaving.append(pltpu.make_async_copy(out_ref.at[:, lanes], out_hbm.at[:, lanes], out_sems.at[len(leaving)]))
        leaving[-1].start()

    leave(2 * LOCAL, 128)
    own_ref[...] = x_ref[pl.ds(pl.multiple_of(my_t * OWN_ROWS, OWN_ROWS), OWN_ROWS), :]

    for which, (codes, scales, base) in enumerate(((gate_codes, gate_scales, 0), (up_codes, up_scales, LOCAL))):
        for block in range(BLOCKS):
            if (which, block) in copies:
                copies[which, block].wait()
            lanes = pl.ds(block * FACTOR, FACTOR)
            word = codes[:, lanes]
            scale = scales[:, lanes].astype(F32)
            if base:
                scale = scale * (2 * signs[lanes].reshape(1, FACTOR) - 1).astype(F32)
            spread = jnp.where(top, scale[0:1, :], scale[1:2, :])
            low = (((word & 15) - 8).astype(F32) * spread).astype(BF16)
            high = (((word >> 4) - 8).astype(F32) * spread).astype(BF16)
            weight = jnp.concatenate([low, high], axis=0)
            part = jnp.dot(ordered, weight, preferred_element_type=F32)
            out_ref[:, pl.ds(base + block * FACTOR, FACTOR)] = part.astype(BF16)
            if block + 1 in ends:
                first = ends[ends.index(block + 1) - 1]
                leave(base + first * FACTOR, (block + 1 - first) * FACTOR)
    for copy in leaving:
        copy.wait()


def rotate_down(codes, scales, out_ref):
    row = lax.broadcasted_iota(jnp.int32, (FACTOR, FACTOR), 0)
    column = lax.broadcasted_iota(jnp.int32, (FACTOR, FACTOR), 1)
    half = FACTOR // 2
    column = jnp.where(column < half, 2 * column, 2 * (column - half) + 1)
    table = parity_sign(row & column).astype(BF16)
    norm = (N_T * FACTOR) ** -0.5
    for block in range(BLOCKS):
        word = codes[pl.ds(block * half, half), :]
        scale = scales[pl.ds(block, 1), :].astype(F32)
        low = (((word & 15) - 8).astype(F32) * scale).astype(BF16)
        high = (((word >> 4) - 8).astype(F32) * scale).astype(BF16)
        weight = jnp.concatenate([low, high], axis=0)
        mixed = jnp.dot(table, weight, preferred_element_type=F32) * norm
        out_ref[pl.ds(block * FACTOR, FACTOR), :] = mixed.astype(BF16)


def sum_near(parts, out_ref, total, joined):
    for block in range(WIDE // 128):
        lanes = pl.ds(block * 128, 128)
        value = parts[0, :, lanes].astype(F32)
        for source in range(1, N_NEAR):
            value = value + parts[source, :, lanes].astype(F32)
        total[:, lanes] = value
    squares = total[:, pl.ds(2 * LOCAL, 1)] + total[:, pl.ds(2 * LOCAL + 1, 1)]
    tail = two_parts(squares, 64)
    for piece in range(N_ZH):
        joined[:, 0:SLICE] = total[:, piece * SLICE : (piece + 1) * SLICE]
        joined[:, SLICE : 2 * SLICE] = total[:, LOCAL + piece * SLICE : LOCAL + (piece + 1) * SLICE]
        joined[:, 2 * SLICE : PIECE] = tail
        value = joined[...].astype(BF16)
        for yh in range(N_YH):
            out_ref[yh * N_ZH + piece] = value[8 * yh : 8 * yh + 8, :]


def source_of(shift):
    return lax.rem(lax.axis_index("zh") + N_ZH - shift, N_ZH)


def activate(parts, out_ref, joined, mixed, ordered):
    values = []
    inverse = None
    for z in range(N_ZH):
        value = parts[z].astype(F32)
        for yh in range(1, N_YH):
            value = value + parts[yh * N_ZH + z].astype(F32)
        joined[...] = value
        if z == 0:
            squares = joined[:, 2 * SLICE : 2 * SLICE + 1] + joined[:, 2 * SLICE + 1 : 2 * SLICE + 2]
            inverse = lax.rsqrt(squares / D + EPSILON)
        gate = joined[:, 0:SLICE] * inverse
        up = joined[:, SLICE : 2 * SLICE] * inverse
        act = gate / (1.0 + jnp.exp(-gate)) * up
        values.append(act.astype(BF16).astype(F32))
    step = 1
    while step < N_ZH:
        values = [
            values[i] + values[i + step] if not i & step else values[i - step] - values[i]
            for i in range(N_ZH)
        ]
        step *= 2
    for z in range(N_ZH):
        mixed[z] = values[z]
    for j in range(N_ZH):
        ordered[:, j * SLICE : (j + 1) * SLICE] = mixed[source_of(j)]
    for block in range(BLOCKS):
        lanes = pl.ds(block * 128, 128)
        value = ordered[:, lanes].astype(BF16)
        for target in range(out_ref.shape[0]):
            out_ref[target, :, lanes] = value


def spread_near(parts, out_ref):
    for yh in range(N_YH):
        value = parts[yh]
        for target in range(N_NEAR):
            out_ref[target, 8 * yh : 8 * yh + 8, :] = value


def project_out(act_ref, own_ref, other_ref, out_ref):
    act = act_ref[...]
    own = jnp.dot(act, own_ref[...], preferred_element_type=F32)
    other = jnp.dot(act, other_ref[...], preferred_element_type=F32)
    out_ref[...] = (own * side("zl") + other).astype(BF16)


def finish(parts, residual, out_ref):
    value = residual[...].astype(F32)
    for t in range(N_T):
        value = value + parts[t].astype(F32)
    value = value.astype(BF16)
    for t in range(N_T):
        out_ref[t] = value


def exchange(blocks, axes):
    return lax.all_to_all(blocks, axes, split_axis=0, concat_axis=0, tiled=True)


def side(axis):
    return (1 - 2 * lax.axis_index(axis)).astype(F32)


def swapped(weight, axis):
    return lax.ppermute(weight, axis, [(0, 1), (1, 0)])


def blend_core(own_ref, other_ref, *out_refs):
    for j in range(N_ZH):
        group = lax.rem(lax.axis_index("zh") + j, N_ZH)
        rows = pl.ds(pl.multiple_of(group * SLICE, SLICE), SLICE)
        both = own_ref[rows, :].astype(F32) * side("c") + other_ref[rows, :].astype(F32)
        out_refs[j][...] = both.astype(BF16)


def join(*refs):
    out_ref = refs[N_ZH]
    for j in range(N_ZH):
        out_ref[pl.ds(j * SLICE, SLICE), :] = refs[j][...]


def shards(residual, norm_gain, gate_codes, gate_scales, up_codes, up_scales, down_codes, down_scales, hidden_signs):
    shape = jax.ShapeDtypeStruct
    columns = residual.shape[1]
    inputs = (residual, norm_gain, gate_codes, gate_scales, up_codes, up_scales, hidden_signs)
    part, own_rows = pl.pallas_call(
        project_in,
        out_shape=[shape((ROWS, WIDE), BF16), shape((OWN_ROWS, columns), BF16)],
        in_specs=[pl.BlockSpec(memory_space=pltpu.HBM)] * len(inputs),
        out_specs=[pl.BlockSpec(memory_space=pltpu.HBM), pl.BlockSpec(memory_space=pltpu.VMEM)],
        scratch_shapes=[pltpu.VMEM((ROWS, WIDE), BF16), pltpu.SemaphoreType.DMA((5,))]
        + [pltpu.VMEM(a.shape, a.dtype) for a in inputs] + [pltpu.SemaphoreType.DMA((7,))],
        compiler_params=pltpu.CompilerParams(vmem_limit_bytes=48 << 20),
    )(*(pltpu.with_memory_space_constraint(a, pltpu.HBM) for a in inputs))
    near = exchange(part.reshape(N_NEAR, NEAR_ROWS, WIDE), NEAR)
    weight = call(rotate_down, shape((LOCAL, columns), BF16))(down_codes, down_scales)
    other = swapped(weight, "c")
    groups = call(blend_core, [shape((SLICE, columns), BF16)] * N_ZH)(weight, other)
    dealt = [groups[0]]
    for j in range(1, N_ZH):
        dealt.append(lax.ppermute(groups[j], "zh", [(i, (i + j) % N_ZH) for i in range(N_ZH)]))
    weight = call(join, shape((LOCAL, columns), BF16))(*dealt)
    other = swapped(weight, "zl")
    scratch = [pltpu.VMEM((NEAR_ROWS, WIDE), F32), pltpu.VMEM((NEAR_ROWS, PIECE), F32)]
    pieces = call(sum_near, shape((N_YH * N_ZH, 8, PIECE), BF16), scratch)(near)
    far = exchange(pieces, FAR)
    scratch = [pltpu.VMEM((8, PIECE), F32), pltpu.VMEM((N_ZH, 8, SLICE), F32), pltpu.VMEM((8, LOCAL), F32)]
    mixed = call(activate, shape((N_YH, 8, LOCAL), BF16), scratch)(far)
    back = exchange(mixed, "yh")
    copies = call(spread_near, shape((N_NEAR, NEAR_ROWS, LOCAL), BF16))(back)
    rotated = exchange(copies, NEAR).reshape(ROWS, LOCAL)
    partial = call(project_out, shape((ROWS, columns), BF16), [])(rotated, weight, other)
    sums = exchange(partial.reshape(N_T, OWN_ROWS, columns), TENSOR)
    out = call(finish, shape((N_T, OWN_ROWS, columns), BF16))(sums, own_rows)
    return exchange(out, TENSOR).reshape(ROWS, columns)


def solution(mesh):
    torus = Mesh(mesh.devices.reshape(4, N_YH, 2, N_ZH, 2, 2), ("x", "yh", "yl", "zh", "zl", "c"))
    pipe = ("x", "yh", "yl")
    placed = (
        P(None, pipe),
        P(pipe),
        P(pipe, TENSOR),
        P(pipe, TENSOR),
        P(pipe, TENSOR),
        P(pipe, TENSOR),
        P(TENSOR, pipe),
        P(TENSOR, pipe),
        P(TENSOR),
    )
    return jax.shard_map(shards, mesh=torus, in_specs=placed, out_specs=P(None, pipe), check_vma=False)
```

```python
import jax
import jax.numpy as jnp
from jax import lax
from jax.experimental import pallas as pl
from jax.experimental.pallas import tpu as pltpu
from jax.sharding import Mesh
from jax.sharding import PartitionSpec as P

D = 8192
ROWS = 256
FACTOR = 128
EPSILON = 1e-05
NEAR = ("yl", "x")
FAR = ("zh", "yh")
TENSOR = ("zh", "zl", "c")
SPREAD = ("c", "zh", "zl")
N_NEAR = 8
N_YH = 4
N_ZH = 4
N_T = 16
LOCAL = 1664
SLICE = LOCAL // N_ZH
BLOCKS = LOCAL // FACTOR
WIDE = 2 * LOCAL + 128
PIECE = 2 * SLICE + 64
NEAR_ROWS = ROWS // N_NEAR
OWN_ROWS = ROWS // N_T
F32 = jnp.float32
BF16 = jnp.bfloat16


def parity_sign(common):
    parity = common
    for shift in (4, 2, 1):
        parity = parity ^ (parity >> shift)
    return (1 - 2 * (parity & 1)).astype(F32)


def call(body, out_shape, scratch=()):
    return pl.pallas_call(
        body,
        out_shape=out_shape,
        scratch_shapes=scratch,
        compiler_params=pltpu.CompilerParams(vmem_limit_bytes=48 << 20),
    )


def two_parts(value, lanes):
    lane = lax.broadcasted_iota(jnp.int32, (value.shape[0], lanes), 1)
    coarse = value.astype(BF16).astype(F32)
    return jnp.where(lane == 0, coarse, jnp.where(lane == 1, value - coarse, 0.0))


def project_in(x_hbm, gain_hbm, gate_hbm, gate_scales_hbm, up_hbm, up_scales_hbm, signs_hbm, out_hbm, own_ref, *scratch):
    out_ref, out_sems, x_ref, gain_ref, gate_codes, gate_scales, up_codes, up_scales, signs, sems = scratch
    small = [
        pltpu.make_async_copy(source, target, sems.at[i])
        for i, (source, target) in enumerate(
            [(x_hbm, x_ref), (gain_hbm, gain_ref), (gate_scales_hbm, gate_scales), (up_scales_hbm, up_scales), (signs_hbm, signs)]
        )
    ]
    for copy in small:
        copy.start()
    copies = {}
    starts = (0, BLOCKS)
    ends = (0, 7, BLOCKS)
    slot = len(small)
    for which, (source, target) in enumerate(((gate_hbm, gate_codes), (up_hbm, up_codes))):
        for first, last in zip(starts[:-1], starts[1:]):
            lanes = pl.ds(first * FACTOR, (last - first) * FACTOR)
            copies[which, first] = pltpu.make_async_copy(source.at[:, lanes], target.at[:, lanes], sems.at[slot])
            copies[which, first].start()
            slot += 1

    width = x_ref.shape[1]
    half = width // 2
    source = lax.broadcasted_iota(jnp.int32, (width, width), 0)
    target = lax.broadcasted_iota(jnp.int32, (width, width), 1)
    wanted = jnp.where(target < half, 2 * target, 2 * (target - half) + 1)
    order = (source == wanted).astype(F32).astype(BF16)
    words = gate_codes.shape[0]
    top = lax.broadcasted_iota(jnp.int32, (words, FACTOR), 0) < words // 2
    my_t = lax.axis_index(SPREAD)
    for copy in small:
        copy.wait()
    wide = x_ref[...].astype(F32)
    scaled = (wide * gain_ref[...].reshape(1, width).astype(F32)).astype(BF16)
    ordered = jnp.dot(scaled, order, preferred_element_type=F32).astype(BF16)
    squares = jnp.sum(wide * wide, axis=1, keepdims=True)
    out_ref[:, pl.ds(2 * LOCAL, 128)] = two_parts(squares, 128).astype(BF16)
    leaving = []

    def leave(first, width):
        lanes = pl.ds(first, width)
        leaving.append(pltpu.make_async_copy(out_ref.at[:, lanes], out_hbm.at[:, lanes], out_sems.at[len(leaving)]))
        leaving[-1].start()

    leave(2 * LOCAL, 128)
    own_ref[...] = x_ref[pl.ds(pl.multiple_of(my_t * OWN_ROWS, OWN_ROWS), OWN_ROWS), :]

    for which, (codes, scales, base) in enumerate(((gate_codes, gate_scales, 0), (up_codes, up_scales, LOCAL))):
        for block in range(BLOCKS):
            if (which, block) in copies:
                copies[which, block].wait()
            lanes = pl.ds(block * FACTOR, FACTOR)
            word = codes[:, lanes]
            scale = scales[:, lanes].astype(F32)
            if base:
                scale = scale * (2 * signs[lanes].reshape(1, FACTOR) - 1).astype(F32)
            spread = jnp.where(top, scale[0:1, :], scale[1:2, :])
            low = (((word & 15) - 8).astype(F32) * spread).astype(BF16)
            high = (((word >> 4) - 8).astype(F32) * spread).astype(BF16)
            weight = jnp.concatenate([low, high], axis=0)
            part = jnp.dot(ordered, weight, preferred_element_type=F32)
            out_ref[:, pl.ds(base + block * FACTOR, FACTOR)] = part.astype(BF16)
            if block + 1 in ends:
                first = ends[ends.index(block + 1) - 1]
                leave(base + first * FACTOR, (block + 1 - first) * FACTOR)
    for copy in leaving:
        copy.wait()


def rotate_down(codes, scales, out_ref):
    row = lax.broadcasted_iota(jnp.int32, (FACTOR, FACTOR), 0)
    column = lax.broadcasted_iota(jnp.int32, (FACTOR, FACTOR), 1)
    half = FACTOR // 2
    column = jnp.where(column < half, 2 * column, 2 * (column - half) + 1)
    table = parity_sign(row & column).astype(BF16)
    norm = (N_T * FACTOR) ** -0.5
    for block in range(BLOCKS):
        word = codes[pl.ds(block * half, half), :]
        scale = scales[pl.ds(block, 1), :].astype(F32)
        low = (((word & 15) - 8).astype(F32) * scale).astype(BF16)
        high = (((word >> 4) - 8).astype(F32) * scale).astype(BF16)
        weight = jnp.concatenate([low, high], axis=0)
        mixed = jnp.dot(table, weight, preferred_element_type=F32) * norm
        out_ref[pl.ds(block * FACTOR, FACTOR), :] = mixed.astype(BF16)


def sum_near(parts, out_ref, total, joined):
    for block in range(WIDE // 128):
        lanes = pl.ds(block * 128, 128)
        value = parts[0, :, lanes].astype(F32)
        for source in range(1, N_NEAR):
            value = value + parts[source, :, lanes].astype(F32)
        total[:, lanes] = value
    squares = total[:, pl.ds(2 * LOCAL, 1)] + total[:, pl.ds(2 * LOCAL + 1, 1)]
    tail = two_parts(squares, 64)
    for piece in range(N_ZH):
        joined[:, 0:SLICE] = total[:, piece * SLICE : (piece + 1) * SLICE]
        joined[:, SLICE : 2 * SLICE] = total[:, LOCAL + piece * SLICE : LOCAL + (piece + 1) * SLICE]
        joined[:, 2 * SLICE : PIECE] = tail
        value = joined[...].astype(BF16)
        for yh in range(N_YH):
            out_ref[piece * N_YH + yh] = value[8 * yh : 8 * yh + 8, :]


def source_of(shift):
    return lax.rem(lax.axis_index("zh") + N_ZH - shift, N_ZH)


def activate(parts, out_ref, joined, mixed, ordered):
    values = []
    inverse = None
    for z in range(N_ZH):
        value = parts[z * N_YH].astype(F32)
        for yh in range(1, N_YH):
            value = value + parts[z * N_YH + yh].astype(F32)
        joined[...] = value
        if z == 0:
            squares = joined[:, 2 * SLICE : 2 * SLICE + 1] + joined[:, 2 * SLICE + 1 : 2 * SLICE + 2]
            inverse = lax.rsqrt(squares / D + EPSILON)
        gate = joined[:, 0:SLICE] * inverse
        up = joined[:, SLICE : 2 * SLICE] * inverse
        act = gate / (1.0 + jnp.exp(-gate)) * up
        values.append(act.astype(BF16).astype(F32))
    step = 1
    while step < N_ZH:
        values = [
            values[i] + values[i + step] if not i & step else values[i - step] - values[i]
            for i in range(N_ZH)
        ]
        step *= 2
    for z in range(N_ZH):
        mixed[z] = values[z]
    for j in range(N_ZH):
        ordered[:, j * SLICE : (j + 1) * SLICE] = mixed[source_of(j)]
    for block in range(BLOCKS):
        lanes = pl.ds(block * 128, 128)
        value = ordered[:, lanes].astype(BF16)
        for target in range(out_ref.shape[0]):
            out_ref[target, :, lanes] = value


def spread_near(parts, out_ref):
    for yh in range(N_YH):
        value = parts[yh]
        for target in range(N_NEAR):
            out_ref[target, 8 * yh : 8 * yh + 8, :] = value


def blend_chip(own_ref, other_ref, out_ref):
    out_ref[...] = (own_ref[...].astype(F32) * side("zl") + other_ref[...].astype(F32)).astype(BF16)


def project_out(act, weight, out_ref):
    out_ref[...] = jnp.dot(act[...], weight[...], preferred_element_type=F32).astype(BF16)


def finish(parts, residual, out_ref):
    value = residual[...].astype(F32)
    for t in range(N_T):
        value = value + parts[t].astype(F32)
    value = value.astype(BF16)
    for t in range(N_T):
        out_ref[t] = value


def exchange(blocks, axes):
    return lax.all_to_all(blocks, axes, split_axis=0, concat_axis=0, tiled=True)


def side(axis):
    return (1 - 2 * lax.axis_index(axis)).astype(F32)


def swapped(weight, axis):
    return lax.ppermute(weight, axis, [(0, 1), (1, 0)])


def blend_core(own_ref, other_ref, *out_refs):
    for j in range(N_ZH):
        group = lax.rem(lax.axis_index("zh") + j, N_ZH)
        rows = pl.ds(pl.multiple_of(group * SLICE, SLICE), SLICE)
        both = own_ref[rows, :].astype(F32) * side("c") + other_ref[rows, :].astype(F32)
        out_refs[j][...] = both.astype(BF16)


def join(*refs):
    out_ref = refs[N_ZH]
    for j in range(N_ZH):
        out_ref[pl.ds(j * SLICE, SLICE), :] = refs[j][...]


def shards(residual, norm_gain, gate_codes, gate_scales, up_codes, up_scales, down_codes, down_scales, hidden_signs):
    shape = jax.ShapeDtypeStruct
    columns = residual.shape[1]
    inputs = (residual, norm_gain, gate_codes, gate_scales, up_codes, up_scales, hidden_signs)
    part, own_rows = pl.pallas_call(
        project_in,
        out_shape=[shape((ROWS, WIDE), BF16), shape((OWN_ROWS, columns), BF16)],
        in_specs=[pl.BlockSpec(memory_space=pltpu.HBM)] * len(inputs),
        out_specs=[pl.BlockSpec(memory_space=pltpu.HBM), pl.BlockSpec(memory_space=pltpu.VMEM)],
        scratch_shapes=[pltpu.VMEM((ROWS, WIDE), BF16), pltpu.SemaphoreType.DMA((5,))]
        + [pltpu.VMEM(a.shape, a.dtype) for a in inputs] + [pltpu.SemaphoreType.DMA((7,))],
        compiler_params=pltpu.CompilerParams(vmem_limit_bytes=48 << 20),
    )(*(pltpu.with_memory_space_constraint(a, pltpu.HBM) for a in inputs))
    near = exchange(part.reshape(N_NEAR, NEAR_ROWS, WIDE), NEAR)
    weight = call(rotate_down, shape((LOCAL, columns), BF16))(down_codes, down_scales)
    other = swapped(weight, "c")
    groups = call(blend_core, [shape((SLICE, columns), BF16)] * N_ZH)(weight, other)
    dealt = [groups[0]]
    for j in range(1, N_ZH):
        dealt.append(lax.ppermute(groups[j], "zh", [(i, (i + j) % N_ZH) for i in range(N_ZH)]))
    weight = call(join, shape((LOCAL, columns), BF16))(*dealt)
    other = swapped(weight, "zl")
    scratch = [pltpu.VMEM((NEAR_ROWS, WIDE), F32), pltpu.VMEM((NEAR_ROWS, PIECE), F32)]
    pieces = call(sum_near, shape((N_YH * N_ZH, 8, PIECE), BF16), scratch)(near)
    far = exchange(pieces, FAR)
    scratch = [pltpu.VMEM((8, PIECE), F32), pltpu.VMEM((N_ZH, 8, SLICE), F32), pltpu.VMEM((8, LOCAL), F32)]
    mixed = call(activate, shape((N_YH, 8, LOCAL), BF16), scratch)(far)
    back = exchange(mixed, "yh")
    copies = call(spread_near, shape((N_NEAR, NEAR_ROWS, LOCAL), BF16))(back)
    rotated = exchange(copies, NEAR).reshape(ROWS, LOCAL)
    weight = call(blend_chip, shape((LOCAL, columns), BF16))(weight, other)
    partial = call(project_out, shape((ROWS, columns), BF16))(rotated, weight)
    sums = exchange(partial.reshape(N_T, OWN_ROWS, columns), SPREAD)
    out = call(finish, shape((N_T, OWN_ROWS, columns), BF16))(sums, own_rows)
    return exchange(out, SPREAD).reshape(ROWS, columns)


def solution(mesh):
    torus = Mesh(mesh.devices.reshape(4, N_YH, 2, N_ZH, 2, 2), ("x", "yh", "yl", "zh", "zl", "c"))
    pipe = ("x", "yh", "yl")
    placed = (
        P(None, pipe),
        P(pipe),
        P(pipe, TENSOR),
        P(pipe, TENSOR),
        P(pipe, TENSOR),
        P(pipe, TENSOR),
        P(TENSOR, pipe),
        P(TENSOR, pipe),
        P(TENSOR),
    )
    return jax.shard_map(shards, mesh=torus, in_specs=placed, out_specs=P(None, pipe), check_vma=False)
```

```python
import jax
import jax.numpy as jnp
from jax import lax
from jax.experimental import pallas as pl
from jax.experimental.pallas import tpu as pltpu
from jax.sharding import Mesh
from jax.sharding import PartitionSpec as P

D = 8192
ROWS = 256
FACTOR = 128
EPSILON = 1e-05
NEAR = ("yl", "x")
FAR = ("zh", "yh")
TENSOR = ("zh", "zl", "c")
SPREAD = ("c", "zh", "zl")
N_NEAR = 8
N_YH = 4
N_ZH = 4
N_T = 16
LOCAL = 1664
SLICE = LOCAL // N_ZH
BLOCKS = LOCAL // FACTOR
TILES = 4 * (2 * LOCAL // 128) + 1
PIECE = 2 * SLICE + 64
NEAR_ROWS = ROWS // N_NEAR
OWN_ROWS = ROWS // N_T
F32 = jnp.float32
BF16 = jnp.bfloat16


def parity_sign(common):
    parity = common
    for shift in (4, 2, 1):
        parity = parity ^ (parity >> shift)
    return (1 - 2 * (parity & 1)).astype(F32)


def call(body, out_shape, scratch=()):
    return pl.pallas_call(
        body,
        out_shape=out_shape,
        scratch_shapes=scratch,
        compiler_params=pltpu.CompilerParams(vmem_limit_bytes=48 << 20),
    )


def two_parts(value, lanes):
    lane = lax.broadcasted_iota(jnp.int32, (value.shape[0], lanes), 1)
    coarse = value.astype(BF16).astype(F32)
    return jnp.where(lane == 0, coarse, jnp.where(lane == 1, value - coarse, 0.0))


def project_in(x_hbm, gain_hbm, gate_hbm, gate_scales_hbm, up_hbm, up_scales_hbm, signs_hbm, out_hbm, own_ref, *scratch):
    out_ref, out_sems, x_ref, gain_ref, gate_codes, gate_scales, up_codes, up_scales, signs, sems = scratch
    small = [
        pltpu.make_async_copy(source, target, sems.at[i])
        for i, (source, target) in enumerate(
            [(x_hbm, x_ref), (gain_hbm, gain_ref), (gate_scales_hbm, gate_scales), (up_scales_hbm, up_scales), (signs_hbm, signs)]
        )
    ]
    for copy in small:
        copy.start()
    copies = {}
    starts = (0, BLOCKS)
    ends = (0, 7, BLOCKS)
    slot = len(small)
    for which, (source, target) in enumerate(((gate_hbm, gate_codes), (up_hbm, up_codes))):
        for first, last in zip(starts[:-1], starts[1:]):
            lanes = pl.ds(first * FACTOR, (last - first) * FACTOR)
            copies[which, first] = pltpu.make_async_copy(source.at[:, lanes], target.at[:, lanes], sems.at[slot])
            copies[which, first].start()
            slot += 1

    width = x_ref.shape[1]
    half = width // 2
    source = lax.broadcasted_iota(jnp.int32, (width, width), 0)
    target = lax.broadcasted_iota(jnp.int32, (width, width), 1)
    wanted = jnp.where(target < half, 2 * target, 2 * (target - half) + 1)
    order = (source == wanted).astype(F32).astype(BF16)
    words = gate_codes.shape[0]
    top = lax.broadcasted_iota(jnp.int32, (words, FACTOR), 0) < words // 2
    my_t = lax.axis_index(SPREAD)
    for copy in small:
        copy.wait()
    wide = x_ref[...].astype(F32)
    scaled = (wide * gain_ref[...].reshape(1, width).astype(F32)).astype(BF16)
    ordered = jnp.dot(scaled, order, preferred_element_type=F32).astype(BF16)
    squares = jnp.sum(wide * wide, axis=1, keepdims=True)
    coarse = squares.astype(BF16).astype(F32)
    both = [jnp.broadcast_to(value, (ROWS, 128)).reshape(N_NEAR, 4, 8, 128) for value in (coarse, squares - coarse)]
    lane = lax.broadcasted_iota(jnp.int32, (N_NEAR, 8, 128), 2)
    tile = jnp.zeros((N_NEAR, 8, 128), F32)
    for place in range(8):
        tile = jnp.where(lane == place, both[place % 2][:, place // 2], tile)
    out_ref[:, TILES - 1] = tile.astype(BF16)
    leaving = []

    def leave(first, width):
        tiles = pl.ds(first, width)
        leaving.append(pltpu.make_async_copy(out_ref.at[:, tiles], out_hbm.at[:, tiles], out_sems.at[len(leaving)]))
        leaving[-1].start()

    leave(TILES - 1, 1)
    own_ref[...] = x_ref[pl.ds(pl.multiple_of(my_t * OWN_ROWS, OWN_ROWS), OWN_ROWS), :]

    for which, (codes, scales, base) in enumerate(((gate_codes, gate_scales, 0), (up_codes, up_scales, LOCAL))):
        for block in range(BLOCKS):
            if (which, block) in copies:
                copies[which, block].wait()
            lanes = pl.ds(block * FACTOR, FACTOR)
            word = codes[:, lanes]
            scale = scales[:, lanes].astype(F32)
            if base:
                scale = scale * (2 * signs[lanes].reshape(1, FACTOR) - 1).astype(F32)
            spread = jnp.where(top, scale[0:1, :], scale[1:2, :])
            low = (((word & 15) - 8).astype(F32) * spread).astype(BF16)
            high = (((word >> 4) - 8).astype(F32) * spread).astype(BF16)
            weight = jnp.concatenate([low, high], axis=0)
            part = jnp.dot(ordered, weight, preferred_element_type=F32)
            column = base // FACTOR + block
            out_ref[:, pl.ds(4 * column, 4)] = part.reshape(N_NEAR, 4, 8, 128).astype(BF16)
            if block + 1 in ends:
                first = ends[ends.index(block + 1) - 1]
                leave(4 * (base // FACTOR + first), 4 * (block + 1 - first))
    for copy in leaving:
        copy.wait()


def rotate_down(codes, scales, out_ref):
    row = lax.broadcasted_iota(jnp.int32, (FACTOR, FACTOR), 0)
    column = lax.broadcasted_iota(jnp.int32, (FACTOR, FACTOR), 1)
    half = FACTOR // 2
    column = jnp.where(column < half, 2 * column, 2 * (column - half) + 1)
    table = parity_sign(row & column).astype(BF16)
    norm = (N_T * FACTOR) ** -0.5
    for block in range(BLOCKS):
        word = codes[pl.ds(block * half, half), :]
        scale = scales[pl.ds(block, 1), :].astype(F32)
        low = (((word & 15) - 8).astype(F32) * scale).astype(BF16)
        high = (((word >> 4) - 8).astype(F32) * scale).astype(BF16)
        weight = jnp.concatenate([low, high], axis=0)
        mixed = jnp.dot(table, weight, preferred_element_type=F32) * norm
        out_ref[pl.ds(block * FACTOR, FACTOR), :] = mixed.astype(BF16)


def sum_near(parts, out_ref, total, joined):
    def summed(first, width):
        value = parts[0, first : first + width].astype(F32)
        for source in range(1, N_NEAR):
            value = value + parts[source, first : first + width].astype(F32)
        return value

    for column in range(2 * BLOCKS):
        total[:, column * 128 : (column + 1) * 128] = summed(4 * column, 4).reshape(NEAR_ROWS, 128)
    tile = summed(TILES - 1, 1).reshape(8, 128)
    squares = jnp.concatenate([tile[:, 2 * i : 2 * i + 1] + tile[:, 2 * i + 1 : 2 * i + 2] for i in range(4)], axis=0)
    tail = two_parts(squares, 64)
    for piece in range(N_ZH):
        joined[:, 0:SLICE] = total[:, piece * SLICE : (piece + 1) * SLICE]
        joined[:, SLICE : 2 * SLICE] = total[:, LOCAL + piece * SLICE : LOCAL + (piece + 1) * SLICE]
        joined[:, 2 * SLICE : PIECE] = tail
        value = joined[...].astype(BF16)
        for yh in range(N_YH):
            out_ref[piece * N_YH + yh] = value[8 * yh : 8 * yh + 8, :]


def source_of(shift):
    return lax.rem(lax.axis_index("zh") + N_ZH - shift, N_ZH)


def activate(parts, out_ref, joined, mixed, ordered):
    values = []
    inverse = None
    for z in range(N_ZH):
        value = parts[z * N_YH].astype(F32)
        for yh in range(1, N_YH):
            value = value + parts[z * N_YH + yh].astype(F32)
        joined[...] = value
        if z == 0:
            squares = joined[:, 2 * SLICE : 2 * SLICE + 1] + joined[:, 2 * SLICE + 1 : 2 * SLICE + 2]
            inverse = lax.rsqrt(squares / D + EPSILON)
        gate = joined[:, 0:SLICE] * inverse
        up = joined[:, SLICE : 2 * SLICE] * inverse
        act = gate / (1.0 + jnp.exp(-gate)) * up
        values.append(act.astype(BF16).astype(F32))
    step = 1
    while step < N_ZH:
        values = [
            values[i] + values[i + step] if not i & step else values[i - step] - values[i]
            for i in range(N_ZH)
        ]
        step *= 2
    for z in range(N_ZH):
        mixed[z] = values[z]
    for j in range(N_ZH):
        ordered[:, j * SLICE : (j + 1) * SLICE] = mixed[source_of(j)]
    for block in range(BLOCKS):
        lanes = pl.ds(block * 128, 128)
        value = ordered[:, lanes].astype(BF16)
        for target in range(out_ref.shape[0]):
            out_ref[target, :, lanes] = value


def spread_near(parts, out_ref):
    for yh in range(N_YH):
        value = parts[yh]
        for target in range(N_NEAR):
            out_ref[target, 8 * yh : 8 * yh + 8, :] = value


def blend_chip(own_ref, other_ref, out_ref):
    out_ref[...] = (own_ref[...].astype(F32) * side("zl") + other_ref[...].astype(F32)).astype(BF16)


def project_out(act, weight, out_ref):
    out_ref[...] = jnp.dot(act[...], weight[...], preferred_element_type=F32).astype(BF16)


def finish(parts, residual, out_ref):
    value = residual[...].astype(F32)
    for t in range(N_T):
        value = value + parts[t].astype(F32)
    value = value.astype(BF16)
    for t in range(N_T):
        out_ref[t] = value


def exchange(blocks, axes):
    return lax.all_to_all(blocks, axes, split_axis=0, concat_axis=0, tiled=True)


def side(axis):
    return (1 - 2 * lax.axis_index(axis)).astype(F32)


def swapped(weight, axis):
    return lax.ppermute(weight, axis, [(0, 1), (1, 0)])


def blend_core(own_ref, other_ref, *out_refs):
    for j in range(N_ZH):
        group = lax.rem(lax.axis_index("zh") + j, N_ZH)
        rows = pl.ds(pl.multiple_of(group * SLICE, SLICE), SLICE)
        both = own_ref[rows, :].astype(F32) * side("c") + other_ref[rows, :].astype(F32)
        out_refs[j][...] = both.astype(BF16)


def join(*refs):
    out_ref = refs[N_ZH]
    for j in range(N_ZH):
        out_ref[pl.ds(j * SLICE, SLICE), :] = refs[j][...]


def shards(residual, norm_gain, gate_codes, gate_scales, up_codes, up_scales, down_codes, down_scales, hidden_signs):
    shape = jax.ShapeDtypeStruct
    columns = residual.shape[1]
    inputs = (residual, norm_gain, gate_codes, gate_scales, up_codes, up_scales, hidden_signs)
    part, own_rows = pl.pallas_call(
        project_in,
        out_shape=[shape((N_NEAR, TILES, 8, 128), BF16), shape((OWN_ROWS, columns), BF16)],
        in_specs=[pl.BlockSpec(memory_space=pltpu.HBM)] * len(inputs),
        out_specs=[pl.BlockSpec(memory_space=pltpu.HBM), pl.BlockSpec(memory_space=pltpu.VMEM)],
        scratch_shapes=[pltpu.VMEM((N_NEAR, TILES, 8, 128), BF16), pltpu.SemaphoreType.DMA((5,))]
        + [pltpu.VMEM(a.shape, a.dtype) for a in inputs] + [pltpu.SemaphoreType.DMA((7,))],
        compiler_params=pltpu.CompilerParams(vmem_limit_bytes=48 << 20),
    )(*(pltpu.with_memory_space_constraint(a, pltpu.HBM) for a in inputs))
    near = exchange(part, NEAR)
    weight = call(rotate_down, shape((LOCAL, columns), BF16))(down_codes, down_scales)
    other = swapped(weight, "c")
    groups = call(blend_core, [shape((SLICE, columns), BF16)] * N_ZH)(weight, other)
    dealt = [groups[0]]
    for j in range(1, N_ZH):
        dealt.append(lax.ppermute(groups[j], "zh", [(i, (i + j) % N_ZH) for i in range(N_ZH)]))
    weight = call(join, shape((LOCAL, columns), BF16))(*dealt)
    other = swapped(weight, "zl")
    scratch = [pltpu.VMEM((NEAR_ROWS, 2 * LOCAL), F32), pltpu.VMEM((NEAR_ROWS, PIECE), F32)]
    pieces = call(sum_near, shape((N_YH * N_ZH, 8, PIECE), BF16), scratch)(near)
    far = exchange(pieces, FAR)
    scratch = [pltpu.VMEM((8, PIECE), F32), pltpu.VMEM((N_ZH, 8, SLICE), F32), pltpu.VMEM((8, LOCAL), F32)]
    mixed = call(activate, shape((N_YH, 8, LOCAL), BF16), scratch)(far)
    back = exchange(mixed, "yh")
    copies = call(spread_near, shape((N_NEAR, NEAR_ROWS, LOCAL), BF16))(back)
    rotated = exchange(copies, NEAR).reshape(ROWS, LOCAL)
    weight = call(blend_chip, shape((LOCAL, columns), BF16))(weight, other)
    partial = call(project_out, shape((ROWS, columns), BF16))(rotated, weight)
    sums = exchange(partial.reshape(N_T, OWN_ROWS, columns), SPREAD)
    out = call(finish, shape((N_T, OWN_ROWS, columns), BF16))(sums, own_rows)
    return exchange(out, SPREAD).reshape(ROWS, columns)


def solution(mesh):
    torus = Mesh(mesh.devices.reshape(4, N_YH, 2, N_ZH, 2, 2), ("x", "yh", "yl", "zh", "zl", "c"))
    pipe = ("x", "yh", "yl")
    placed = (
        P(None, pipe),
        P(pipe),
        P(pipe, TENSOR),
        P(pipe, TENSOR),
        P(pipe, TENSOR),
        P(pipe, TENSOR),
        P(TENSOR, pipe),
        P(TENSOR, pipe),
        P(TENSOR),
    )
    return jax.shard_map(shards, mesh=torus, in_specs=placed, out_specs=P(None, pipe), check_vma=False)
```

```python
import jax
import jax.numpy as jnp
from jax import lax
from jax.experimental import pallas as pl
from jax.experimental.pallas import tpu as pltpu
from jax.sharding import Mesh
from jax.sharding import PartitionSpec as P

D = 8192
ROWS = 256
FACTOR = 128
EPSILON = 1e-05
NEAR = ("yl", "x")
FAR = ("zh", "yh")
TENSOR = ("zh", "zl", "c")
SPREAD = ("c", "zh", "zl")
N_NEAR = 8
N_YH = 4
N_ZH = 4
N_T = 16
LOCAL = 1664
SLICE = LOCAL // N_ZH
BLOCKS = LOCAL // FACTOR
TILES = 4 * (2 * LOCAL // 128) + 1
PIECE = 2 * SLICE + 64
NEAR_ROWS = ROWS // N_NEAR
OWN_ROWS = ROWS // N_T
F32 = jnp.float32
BF16 = jnp.bfloat16


def parity_sign(common):
    parity = common
    for shift in (4, 2, 1):
        parity = parity ^ (parity >> shift)
    return (1 - 2 * (parity & 1)).astype(F32)


def call(body, out_shape, scratch=()):
    return pl.pallas_call(
        body,
        out_shape=out_shape,
        scratch_shapes=scratch,
        compiler_params=pltpu.CompilerParams(vmem_limit_bytes=48 << 20),
    )


def two_parts(value, lanes):
    lane = lax.broadcasted_iota(jnp.int32, (value.shape[0], lanes), 1)
    coarse = value.astype(BF16).astype(F32)
    return jnp.where(lane == 0, coarse, jnp.where(lane == 1, value - coarse, 0.0))


def project_in(x_hbm, gain_hbm, gate_hbm, gate_scales_hbm, up_hbm, up_scales_hbm, signs_hbm, out_hbm, own_ref, *scratch):
    out_ref, out_sems, x_ref, gain_ref, gate_codes, gate_scales, up_codes, up_scales, signs, sems = scratch
    small = [
        pltpu.make_async_copy(source, target, sems.at[i])
        for i, (source, target) in enumerate(
            [(x_hbm, x_ref), (gain_hbm, gain_ref), (gate_scales_hbm, gate_scales), (up_scales_hbm, up_scales), (signs_hbm, signs)]
        )
    ]
    for copy in small:
        copy.start()
    copies = {}
    starts = (0, BLOCKS)
    ends = (0, 7, BLOCKS)
    slot = len(small)
    for which, (source, target) in enumerate(((gate_hbm, gate_codes), (up_hbm, up_codes))):
        for first, last in zip(starts[:-1], starts[1:]):
            lanes = pl.ds(first * FACTOR, (last - first) * FACTOR)
            copies[which, first] = pltpu.make_async_copy(source.at[:, lanes], target.at[:, lanes], sems.at[slot])
            copies[which, first].start()
            slot += 1

    width = x_ref.shape[1]
    half = width // 2
    source = lax.broadcasted_iota(jnp.int32, (width, width), 0)
    target = lax.broadcasted_iota(jnp.int32, (width, width), 1)
    wanted = jnp.where(target < half, 2 * target, 2 * (target - half) + 1)
    order = (source == wanted).astype(F32).astype(BF16)
    words = gate_codes.shape[0]
    top = lax.broadcasted_iota(jnp.int32, (words, FACTOR), 0) < words // 2
    my_t = lax.axis_index(SPREAD)
    for copy in small:
        copy.wait()
    wide = x_ref[...].astype(F32)
    scaled = (wide * gain_ref[...].reshape(1, width).astype(F32)).astype(BF16)
    ordered = jnp.dot(scaled, order, preferred_element_type=F32).astype(BF16)
    squares = jnp.sum(wide * wide, axis=1, keepdims=True)
    coarse = squares.astype(BF16).astype(F32)
    both = [jnp.broadcast_to(value, (ROWS, 128)).reshape(N_NEAR, 4, 8, 128) for value in (coarse, squares - coarse)]
    lane = lax.broadcasted_iota(jnp.int32, (N_NEAR, 8, 128), 2)
    tile = jnp.zeros((N_NEAR, 8, 128), F32)
    for place in range(8):
        tile = jnp.where(lane == place, both[place % 2][:, place // 2], tile)
    out_ref[:, TILES - 1] = tile.astype(BF16)
    leaving = []

    def leave(first, width):
        tiles = pl.ds(first, width)
        leaving.append(pltpu.make_async_copy(out_ref.at[:, tiles], out_hbm.at[:, tiles], out_sems.at[len(leaving)]))
        leaving[-1].start()

    leave(TILES - 1, 1)
    own_ref[...] = x_ref[pl.ds(pl.multiple_of(my_t * OWN_ROWS, OWN_ROWS), OWN_ROWS), :]

    for which, (codes, scales, base) in enumerate(((gate_codes, gate_scales, 0), (up_codes, up_scales, LOCAL))):
        for block in range(BLOCKS):
            if (which, block) in copies:
                copies[which, block].wait()
            lanes = pl.ds(block * FACTOR, FACTOR)
            word = codes[:, lanes]
            scale = scales[:, lanes].astype(F32)
            if base:
                scale = scale * (2 * signs[lanes].reshape(1, FACTOR) - 1).astype(F32)
            spread = jnp.where(top, scale[0:1, :], scale[1:2, :])
            low = (((word & 15) - 8).astype(F32) * spread).astype(BF16)
            high = (((word >> 4) - 8).astype(F32) * spread).astype(BF16)
            weight = jnp.concatenate([low, high], axis=0)
            part = jnp.dot(ordered, weight, preferred_element_type=F32)
            column = base // FACTOR + block
            out_ref[:, pl.ds(4 * column, 4)] = part.reshape(N_NEAR, 4, 8, 128).astype(BF16)
            if block + 1 in ends:
                first = ends[ends.index(block + 1) - 1]
                leave(4 * (base // FACTOR + first), 4 * (block + 1 - first))
    for copy in leaving:
        copy.wait()


def rotate_down(codes, scales, out_ref):
    row = lax.broadcasted_iota(jnp.int32, (FACTOR, FACTOR), 0)
    column = lax.broadcasted_iota(jnp.int32, (FACTOR, FACTOR), 1)
    half = FACTOR // 2
    column = jnp.where(column < half, 2 * column, 2 * (column - half) + 1)
    table = parity_sign(row & column).astype(BF16)
    norm = (N_T * FACTOR) ** -0.5
    for block in range(BLOCKS):
        word = codes[pl.ds(block * half, half), :]
        scale = scales[pl.ds(block, 1), :].astype(F32)
        low = (((word & 15) - 8).astype(F32) * scale).astype(BF16)
        high = (((word >> 4) - 8).astype(F32) * scale).astype(BF16)
        weight = jnp.concatenate([low, high], axis=0)
        mixed = jnp.dot(table, weight, preferred_element_type=F32) * norm
        out_ref[pl.ds(block * FACTOR, FACTOR), :] = mixed.astype(BF16)


def sum_near(parts, out_hbm, total, joined, ready, sems):
    def summed(first, width):
        value = parts[0, first : first + width].astype(F32)
        for source in range(1, N_NEAR):
            value = value + parts[source, first : first + width].astype(F32)
        return value

    for column in range(2 * BLOCKS):
        total[:, column * 128 : (column + 1) * 128] = summed(4 * column, 4).reshape(NEAR_ROWS, 128)
    tile = summed(TILES - 1, 1).reshape(8, 128)
    squares = jnp.concatenate([tile[:, 2 * i : 2 * i + 1] + tile[:, 2 * i + 1 : 2 * i + 2] for i in range(4)], axis=0)
    tail = two_parts(squares, 64)
    leaving = []
    for piece in range(N_ZH):
        joined[:, 0:SLICE] = total[:, piece * SLICE : (piece + 1) * SLICE]
        joined[:, SLICE : 2 * SLICE] = total[:, LOCAL + piece * SLICE : LOCAL + (piece + 1) * SLICE]
        joined[:, 2 * SLICE : PIECE] = tail
        ready[piece] = joined[...].reshape(N_YH, 8, PIECE).astype(BF16)
        leaving.append(pltpu.make_async_copy(ready.at[piece], out_hbm.at[pl.ds(piece * N_YH, N_YH)], sems.at[piece]))
        leaving[-1].start()
    for copy in leaving:
        copy.wait()


def source_of(shift):
    return lax.rem(lax.axis_index("zh") + N_ZH - shift, N_ZH)


def activate(parts, out_ref, joined, mixed, ordered):
    values = []
    inverse = None
    for z in range(N_ZH):
        value = parts[z * N_YH].astype(F32)
        for yh in range(1, N_YH):
            value = value + parts[z * N_YH + yh].astype(F32)
        joined[...] = value
        if z == 0:
            squares = joined[:, 2 * SLICE : 2 * SLICE + 1] + joined[:, 2 * SLICE + 1 : 2 * SLICE + 2]
            inverse = lax.rsqrt(squares / D + EPSILON)
        gate = joined[:, 0:SLICE] * inverse
        up = joined[:, SLICE : 2 * SLICE] * inverse
        act = gate / (1.0 + jnp.exp(-gate)) * up
        values.append(act.astype(BF16).astype(F32))
    step = 1
    while step < N_ZH:
        values = [
            values[i] + values[i + step] if not i & step else values[i - step] - values[i]
            for i in range(N_ZH)
        ]
        step *= 2
    for z in range(N_ZH):
        mixed[z] = values[z]
    for j in range(N_ZH):
        ordered[:, j * SLICE : (j + 1) * SLICE] = mixed[source_of(j)]
    for block in range(BLOCKS):
        lanes = pl.ds(block * 128, 128)
        value = ordered[:, lanes].astype(BF16)
        for target in range(out_ref.shape[0]):
            out_ref[target, :, lanes] = value


def spread_near(parts, out_ref):
    for yh in range(N_YH):
        value = parts[yh]
        for target in range(N_NEAR):
            out_ref[target, 8 * yh : 8 * yh + 8, :] = value


def blend_chip(own_ref, other_ref, out_ref):
    out_ref[...] = (own_ref[...].astype(F32) * side("zl") + other_ref[...].astype(F32)).astype(BF16)


def project_out(act, weight, out_ref):
    out_ref[...] = jnp.dot(act[...], weight[...], preferred_element_type=F32).astype(BF16)


def finish(parts, residual, out_ref):
    value = residual[...].astype(F32)
    for t in range(N_T):
        value = value + parts[t].astype(F32)
    value = value.astype(BF16)
    for t in range(N_T):
        out_ref[t] = value


def exchange(blocks, axes):
    return lax.all_to_all(blocks, axes, split_axis=0, concat_axis=0, tiled=True)


def side(axis):
    return (1 - 2 * lax.axis_index(axis)).astype(F32)


def swapped(weight, axis):
    return lax.ppermute(weight, axis, [(0, 1), (1, 0)])


def blend_core(own_ref, other_ref, *out_refs):
    for j in range(N_ZH):
        group = lax.rem(lax.axis_index("zh") + j, N_ZH)
        rows = pl.ds(pl.multiple_of(group * SLICE, SLICE), SLICE)
        both = own_ref[rows, :].astype(F32) * side("c") + other_ref[rows, :].astype(F32)
        out_refs[j][...] = both.astype(BF16)


def join(*refs):
    out_ref = refs[N_ZH]
    for j in range(N_ZH):
        out_ref[pl.ds(j * SLICE, SLICE), :] = refs[j][...]


def shards(residual, norm_gain, gate_codes, gate_scales, up_codes, up_scales, down_codes, down_scales, hidden_signs):
    shape = jax.ShapeDtypeStruct
    columns = residual.shape[1]
    inputs = (residual, norm_gain, gate_codes, gate_scales, up_codes, up_scales, hidden_signs)
    part, own_rows = pl.pallas_call(
        project_in,
        out_shape=[shape((N_NEAR, TILES, 8, 128), BF16), shape((OWN_ROWS, columns), BF16)],
        in_specs=[pl.BlockSpec(memory_space=pltpu.HBM)] * len(inputs),
        out_specs=[pl.BlockSpec(memory_space=pltpu.HBM), pl.BlockSpec(memory_space=pltpu.VMEM)],
        scratch_shapes=[pltpu.VMEM((N_NEAR, TILES, 8, 128), BF16), pltpu.SemaphoreType.DMA((5,))]
        + [pltpu.VMEM(a.shape, a.dtype) for a in inputs] + [pltpu.SemaphoreType.DMA((7,))],
        compiler_params=pltpu.CompilerParams(vmem_limit_bytes=48 << 20),
    )(*(pltpu.with_memory_space_constraint(a, pltpu.HBM) for a in inputs))
    near = exchange(part, NEAR)
    weight = call(rotate_down, shape((LOCAL, columns), BF16))(down_codes, down_scales)
    other = swapped(weight, "c")
    groups = call(blend_core, [shape((SLICE, columns), BF16)] * N_ZH)(weight, other)
    dealt = [groups[0]]
    for j in range(1, N_ZH):
        dealt.append(lax.ppermute(groups[j], "zh", [(i, (i + j) % N_ZH) for i in range(N_ZH)]))
    weight = call(join, shape((LOCAL, columns), BF16))(*dealt)
    other = swapped(weight, "zl")
    scratch = [pltpu.VMEM((NEAR_ROWS, 2 * LOCAL), F32), pltpu.VMEM((NEAR_ROWS, PIECE), F32)]
    scratch += [pltpu.VMEM((N_ZH, N_YH, 8, PIECE), BF16), pltpu.SemaphoreType.DMA((N_ZH,))]
    pieces = pl.pallas_call(
        sum_near,
        out_shape=shape((N_ZH * N_YH, 8, PIECE), BF16),
        out_specs=pl.BlockSpec(memory_space=pltpu.HBM),
        scratch_shapes=scratch,
        compiler_params=pltpu.CompilerParams(vmem_limit_bytes=48 << 20),
    )(near)
    far = exchange(pieces, FAR)
    scratch = [pltpu.VMEM((8, PIECE), F32), pltpu.VMEM((N_ZH, 8, SLICE), F32), pltpu.VMEM((8, LOCAL), F32)]
    mixed = call(activate, shape((N_YH, 8, LOCAL), BF16), scratch)(far)
    back = exchange(mixed, "yh")
    copies = call(spread_near, shape((N_NEAR, NEAR_ROWS, LOCAL), BF16))(back)
    rotated = exchange(copies, NEAR).reshape(ROWS, LOCAL)
    weight = call(blend_chip, shape((LOCAL, columns), BF16))(weight, other)
    partial = call(project_out, shape((ROWS, columns), BF16))(rotated, weight)
    sums = exchange(partial.reshape(N_T, OWN_ROWS, columns), SPREAD)
    out = call(finish, shape((N_T, OWN_ROWS, columns), BF16))(sums, own_rows)
    return exchange(out, SPREAD).reshape(ROWS, columns)


def solution(mesh):
    torus = Mesh(mesh.devices.reshape(4, N_YH, 2, N_ZH, 2, 2), ("x", "yh", "yl", "zh", "zl", "c"))
    pipe = ("x", "yh", "yl")
    placed = (
        P(None, pipe),
        P(pipe),
        P(pipe, TENSOR),
        P(pipe, TENSOR),
        P(pipe, TENSOR),
        P(pipe, TENSOR),
        P(TENSOR, pipe),
        P(TENSOR, pipe),
        P(TENSOR),
    )
    return jax.shard_map(shards, mesh=torus, in_specs=placed, out_specs=P(None, pipe), check_vma=False)
```
